32 devices in a mesh: tm: 16 (over z, y, x), space: 2 (over core).
Axes of the slice: x: 2, y: 2, z: 4, core: 2. Of those that a mesh axis runs over, the one named last changes fastest.
Arguments:
- features: bfloat16 [16, 16, 16, 256], P('tm', 'space'), may hold values from -6 to 6
- masks: int32 [16, 16, 16], P('tm', 'space'), may hold values from 0 to 1
- w_pix: bfloat16 [256, 256], replicated, may hold values from -0.375 to 0.375
- mask_embed: bfloat16 [256], replicated, may hold values from -4 to 4
- w_conv: bfloat16 [3, 3, 256, 256], replicated, may hold values from -0.125 to 0.125
- w_out: bfloat16 [256, 64], replicated, may hold values from -0.375 to 0.375
- w_ptr: bfloat16 [256, 256], replicated, may hold values from -0.375 to 0.375
- w_query: bfloat16 [256, 256], replicated, may hold values from -1 to 1
- w_key: bfloat16 [64, 256], replicated, may hold values from -0.75 to 0.75
- w_value: bfloat16 [64, 256], replicated, may hold values from -0.75 to 0.75
- w_proj: bfloat16 [256, 256], replicated, may hold values from -0.375 to 0.375
- mem_tpos: bfloat16 [3, 64], replicated, may hold values from -120 to 120
- ptr_tpos: bfloat16 [16, 256], replicated, may hold values from -4 to 4
- empty_memory: bfloat16 [64], replicated, may hold values from -4 to 4
Outputs:
- attended: bfloat16 [16, 16, 16, 256], P('tm', 'space')
- memory: bfloat16 [16, 16, 1024], P('tm', 'space')
- pointers: bfloat16 [16, 256], P('tm')
The draws below stay inside these ranges and needn't reach their ends.
All inputs are finite; a program needn't handle non-finite values.
Results may differ from the reference program's by a relative error of at most 0.015.
The reference program's roundings to bfloat16 on the way count: a program that leaves them out, or rounds other values in their place, can miss the bound.
Values may be sent and summed in bfloat16 or wider, within the bound.
A program may use at most 128 MiB of HBM per device.

```python
import jax
import jax.numpy as jnp
from jax import lax

D = 256
MEM_DIM = 64
MEMS = 3
POINTERS = 16
GRID = 16
FRAMES = 16


def draw_masks(key, part):
    first_key, second_key = jax.random.split(key)
    density = jax.random.randint(first_key, (FRAMES, 1, 1), 16, 81)
    row_index = jnp.arange(GRID, dtype=jnp.int32).reshape(1, GRID, 1)
    threshold = density * (GRID + 2 * row_index) // GRID
    cell_draws = jax.random.randint(second_key, (FRAMES, GRID, GRID), 0, 256)
    return (cell_draws < threshold).astype(jnp.int32)


def draw_mem_tpos(key, part):
    drawn = jnp.clip(jax.random.normal(key, (MEMS, MEM_DIM), jnp.float32), -4.0, 4.0)
    return drawn.astype(jnp.bfloat16)


def steps_of(rng, shape, cuts, smallest, largest):
    def one(position, shards_of):
        draws = jax.random.uniform(jax.random.fold_in(jax.random.fold_in(rng, 6), position), (shards_of,), jnp.float32, smallest / len(cuts), largest / len(cuts))
        return jnp.repeat(jnp.exp(draws), shape[position] // shards_of).reshape((-1,) + (1,) * (len(shape) - position - 1))

    loudness = one(*cuts[0])
    for cut in cuts[1:]:
        loudness = loudness * one(*cut)
    return loudness


def bell_draw(rng, dims, scale, bound, cuts=(), kind=jnp.bfloat16):
    result = jax.random.normal(rng, dims, jnp.float32) * scale
    if len(cuts) > 0:
        result = steps_of(rng, dims, cuts, -0.22, 0.18) * result
    return jnp.clip(result, min=-bound, max=bound).astype(kind)


def setup_inputs(seed: int = 0) -> dict:
    keys = jax.random.split(jax.random.key(seed), 15)
    features = bell_draw(keys[0], (FRAMES, GRID, GRID, D), 1.0, 6.0, ((0, 16), (1, 2)))
    masks = draw_masks(jax.random.fold_in(keys[14], 71), 0)
    w_pix = bell_draw(keys[2], (D, D), D ** -0.5, 0.375)
    mask_embed = bell_draw(keys[3], (D,), 1.0, 4.0)
    w_conv = bell_draw(keys[4], (3, 3, D, D), (9 * D) ** -0.5, 0.125)
    w_out = bell_draw(keys[5], (D, MEM_DIM), D ** -0.5, 0.375)
    w_ptr = bell_draw(keys[6], (D, D), D ** -0.5, 0.375)
    w_query = bell_draw(keys[7], (D, D), (D // 9) ** -0.5, 1.0)
    w_key = bell_draw(keys[8], (MEM_DIM, D), MEM_DIM ** -0.5, 0.75)
    w_value = bell_draw(keys[9], (MEM_DIM, D), MEM_DIM ** -0.5, 0.75)
    w_proj = bell_draw(keys[10], (D, D), D ** -0.5, 0.375)
    mem_tpos = draw_mem_tpos(jax.random.fold_in(keys[14], 71), 0)
    ptr_tpos = bell_draw(keys[12], (POINTERS, D), 1.0, 4.0)
    empty_memory = bell_draw(keys[13], (MEM_DIM,), 1.0, 4.0)
    return {"features": features, "masks": masks, "w_pix": w_pix, "mask_embed": mask_embed, "w_conv": w_conv, "w_out": w_out, "w_ptr": w_ptr, "w_query": w_query, "w_key": w_key, "w_value": w_value, "w_proj": w_proj, "mem_tpos": mem_tpos, "ptr_tpos": ptr_tpos, "empty_memory": empty_memory}


def reference(features, masks, w_pix, mask_embed, w_conv, w_out, w_ptr, w_query, w_key, w_value, w_proj, mem_tpos, ptr_tpos, empty_memory):
    ptr_tok = D // MEM_DIM
    tokens = GRID * GRID
    flat_rows = features.reshape(FRAMES * tokens, D)
    mask_rows = masks.reshape(FRAMES * tokens, 1).astype(jnp.float32)
    joined_map = (jnp.dot(flat_rows, w_pix, preferred_element_type=jnp.float32) + mask_rows * mask_embed.astype(jnp.float32)).astype(jnp.bfloat16)
    joined_map = joined_map.reshape(FRAMES, GRID, GRID, D)
    padded = jnp.pad(joined_map, ((0, 0), (1, 1), (1, 1), (0, 0)))
    conv_sum = jnp.zeros((FRAMES * tokens, D), jnp.float32)
    for row_tap in range(3):
        for col_tap in range(3):
            window_rows = padded[:, row_tap:row_tap + GRID, col_tap:col_tap + GRID, :].reshape(-1, D)
            conv_sum = conv_sum + jnp.dot(window_rows, w_conv[row_tap, col_tap], preferred_element_type=jnp.float32)
    hidden = jax.nn.gelu(conv_sum, approximate=True).astype(jnp.bfloat16)
    memory = jnp.dot(hidden, w_out, preferred_element_type=jnp.float32).astype(jnp.bfloat16)
    memory = memory.reshape(FRAMES, GRID, GRID * MEM_DIM)
    pooled = jnp.einsum('ft,ftd->fd', masks.reshape(FRAMES, tokens).astype(jnp.float32), features.reshape(FRAMES, tokens, D).astype(jnp.float32))
    normed = (pooled * lax.rsqrt(lax.optimization_barrier(jnp.mean(pooled * pooled, axis=1, keepdims=True)) + 1e-06)).astype(jnp.bfloat16)
    pointers = jnp.dot(normed, w_ptr, preferred_element_type=jnp.float32).astype(jnp.bfloat16)
    mem_tokens = memory.reshape(FRAMES * tokens, MEM_DIM)
    key_base = jnp.dot(mem_tokens, w_key, preferred_element_type=jnp.float32).reshape(FRAMES, tokens, D)
    all_values = jnp.dot(mem_tokens, w_value, preferred_element_type=jnp.float32).astype(jnp.bfloat16).reshape(FRAMES, tokens, D)
    tpos_keys = jnp.dot(mem_tpos, w_key, preferred_element_type=jnp.float32)
    ptr_tpos_keys = jnp.dot(ptr_tpos[::-1].reshape(POINTERS * ptr_tok, MEM_DIM), w_key, preferred_element_type=jnp.float32)
    null_key = jnp.dot(empty_memory.reshape(1, MEM_DIM), w_key, preferred_element_type=jnp.float32).astype(jnp.bfloat16)
    null_value = jnp.dot(empty_memory.reshape(1, MEM_DIM), w_value, preferred_element_type=jnp.float32).astype(jnp.bfloat16)
    padded_ptr = jnp.concatenate([jnp.zeros((POINTERS, D), jnp.bfloat16), pointers], axis=0)
    ptr_offsets = jnp.repeat(jnp.arange(POINTERS, dtype=jnp.int32) - POINTERS, ptr_tok)
    features_f = features.reshape(FRAMES, tokens, D).astype(jnp.float32)
    centred = features_f - lax.optimization_barrier(jnp.mean(features_f, axis=2, keepdims=True))
    query_in = (centred * lax.rsqrt(lax.optimization_barrier(jnp.mean(centred * centred, axis=2, keepdims=True)) + 1e-05)).astype(jnp.bfloat16)
    queries_all = (jnp.dot(query_in.reshape(-1, D), w_query, preferred_element_type=jnp.float32) * D ** (-0.5)).astype(jnp.bfloat16)
    queries_all = queries_all.reshape(FRAMES, tokens, D)

    def attend_frame(frame):
        key_list = []
        value_list = []
        valid_list = []
        for distance in range(1, MEMS + 1):
            source = jnp.maximum(frame - distance, 0).astype(jnp.int32)
            key_list.append((key_base[source] + tpos_keys[distance - 1]).astype(jnp.bfloat16))
            value_list.append(all_values[source])
            valid_list.append(jnp.broadcast_to(frame - distance >= 0, (tokens,)))
        window = lax.dynamic_slice_in_dim(padded_ptr, frame.astype(jnp.int32), POINTERS, 0)
        ptr_tokens = window.reshape(POINTERS * ptr_tok, MEM_DIM)
        key_list.append((jnp.dot(ptr_tokens, w_key, preferred_element_type=jnp.float32) + ptr_tpos_keys).astype(jnp.bfloat16))
        value_list.append(jnp.dot(ptr_tokens, w_value, preferred_element_type=jnp.float32).astype(jnp.bfloat16))
        valid_list.append(frame + ptr_offsets >= 0)
        key_list.append(null_key)
        value_list.append(null_value)
        valid_list.append(jnp.ones((1,), bool))
        key_rows = jnp.concatenate(key_list, axis=0)
        value_rows = jnp.concatenate(value_list, axis=0)
        is_valid = jnp.concatenate(valid_list, axis=0)
        scores = lax.dot_general(queries_all[frame], key_rows, (((1,), (1,)), ((), ())), preferred_element_type=jnp.float32)
        scores = jnp.where(is_valid[None, :], scores, -jnp.inf)
        row_top = lax.optimization_barrier(jnp.max(scores, axis=1, keepdims=True))
        expo = jnp.exp(scores - row_top)
        weights = (expo / lax.optimization_barrier(jnp.sum(expo, axis=1, keepdims=True))).astype(jnp.bfloat16)
        mixed_rows = jnp.dot(weights, value_rows, preferred_element_type=jnp.float32).astype(jnp.bfloat16)
        return (features_f[frame] + jnp.dot(mixed_rows, w_proj, preferred_element_type=jnp.float32)).astype(jnp.bfloat16)
    attended = lax.map(attend_frame, jnp.arange(FRAMES, dtype=jnp.int32)).reshape(FRAMES, GRID, GRID, D)
    return (attended, memory, pointers)
```

```python
import functools

import jax
import jax.numpy as jnp
from jax import lax
from jax.experimental import pallas as pl
from jax.experimental.pallas import tpu as pltpu
from jax.sharding import PartitionSpec as P

MEMS = 3
POINTERS = 16
MESH = pl.DeviceIdType.MESH
F32 = jnp.float32
BF16 = jnp.bfloat16


def mm(a, b):
    return jnp.dot(a, b, preferred_element_type=F32)


def mm_t(a, b):
    return lax.dot_general(a, b, (((1,), (1,)), ((), ())), preferred_element_type=F32)


def kernel(
    frames,
    features,
    masks,
    mask_embed,
    mem_tpos,
    ptr_tpos,
    empty_memory,
    w_pix,
    w_conv,
    w_out_t,
    w_ptr,
    w_query,
    w_key,
    w_value,
    w_proj,
    attended,
    memory,
    pointers,
    feat,
    pix,
    taps,
    outw,
    ptrw,
    queryw,
    key_pad,
    value_pad,
    projw,
    joined,
    halo,
    conv,
    part,
    part_in,
    mem_rows,
    mem_send,
    mem_in,
    ptr_send,
    ptr_in,
    scores,
    values,
    load_sem,
    near_send,
    near_recv,
    mem_send_sem,
    mem_recv_sem,
    ptr_send_sem,
    ptr_recv_sem,
):
    _, rows, columns, dim = features.shape
    tokens = rows * columns
    mem_dim = w_key.shape[0]
    half = tokens // 2
    parts = dim // mem_dim
    t = lax.axis_index("tm")
    s = lax.axis_index("space")
    other = 1 - s
    reach = min(POINTERS, frames - 1)
    mem_reach = min(MEMS, frames - 1)

    barrier = pltpu.get_barrier_semaphore()
    pl.semaphore_signal(barrier, inc=1, device_id=(t, other), device_id_type=MESH)
    for d in range(reach, 0, -1):

        @pl.when(t - d >= 0)
        def _(d=d):
            pl.semaphore_signal(barrier, inc=1, device_id=(t - d, s), device_id_type=MESH)
            if d <= mem_reach:
                pl.semaphore_signal(
                    barrier, inc=1, device_id=(t - d, other), device_id_type=MESH
                )

    loads = []

    def load(src, dst):
        copy = pltpu.make_async_copy(src, dst, load_sem.at[len(loads)])
        copy.start()
        loads.append(copy)
        return copy

    feat_load = load(features.at[0], feat)
    pix_load = load(w_pix, pix)
    tap_loads = [load(w_conv.at[a], taps.at[a]) for a in range(3)]
    query_load = load(w_query, queryw)
    ptr_load = load(w_ptr, ptrw)
    out_loads = [load(w_out_t, outw.at[pl.ds(k * mem_dim, mem_dim)]) for k in range(2)]
    key_load = load(w_key, key_pad.at[pl.ds(mem_dim, mem_dim)])
    value_load = load(w_value, value_pad.at[pl.ds(mem_dim, mem_dim)])
    proj_load = load(w_proj, projw)

    blank = jnp.zeros((mem_dim, dim), BF16)
    for ref in (key_pad, value_pad):
        ref[0:mem_dim] = blank
        ref[2 * mem_dim : 3 * mem_dim] = blank
    joined[0] = jnp.zeros((columns, dim), BF16)
    joined[rows + 1] = jnp.zeros((columns, dim), BF16)
    for d in range(1, MEMS + 1):

        @pl.when(t - d < 0)
        def _(d=d):
            mem_in[d - 1] = jnp.zeros((2, half, 2 * mem_dim), BF16)

    for d in range(1, POINTERS + 1):

        @pl.when(t - d < 0)
        def _(d=d):
            ptr_in[d - 1] = jnp.zeros((1, dim), F32)

    mask_f = masks[0].astype(F32)
    spread = jnp.concatenate(
        [jnp.broadcast_to(mask_f[r : r + 1], (columns, columns)) for r in range(rows)], axis=0
    )
    token_col = lax.broadcasted_iota(jnp.int32, (tokens, columns), 0) % columns
    lane_col = lax.broadcasted_iota(jnp.int32, (tokens, columns), 1)
    mask_col = jnp.sum(jnp.where(token_col == lane_col, spread, 0.0), axis=1, keepdims=True)
    col_of = lax.broadcasted_iota(jnp.int32, (tokens, dim), 0) % columns

    feat_load.wait()
    flat = feat[...].reshape(tokens, dim)
    flat_f = flat.astype(F32)
    part[...] = jnp.sum(mask_col * flat_f, axis=0, keepdims=True)
    pix_load.wait()
    joined_rows = (
        mm(flat, pix[...]) + mask_col * mask_embed[...].astype(F32).reshape(1, dim)
    ).astype(BF16)
    joined[1 : rows + 1] = joined_rows.reshape(rows, columns, dim)

    sums = [None, None, None]
    for a in range(3):
        tap_loads[a].wait()
        window = joined[a : a + rows].reshape(tokens, dim)
        for b in range(3):
            product = mm(window, taps[a, b])
            sums[b] = product if sums[b] is None else sums[b] + product

    def shift_columns(low, mid, high, col):
        count = low.shape[0]
        low = jnp.where(col == 0, 0.0, pltpu.roll(low, 1, 0))
        high = jnp.where(col == columns - 1, 0.0, pltpu.roll(high, count - 1, 0))
        return mid + low + high

    conv[...] = shift_columns(*sums, col_of)

    centred = flat_f - jnp.mean(flat_f, axis=1, keepdims=True)
    query_in = (
        centred * lax.rsqrt(jnp.mean(centred * centred, axis=1, keepdims=True) + 1e-05)
    ).astype(BF16)
    query_load.wait()
    query = (mm(query_in, queryw[...]) * dim ** (-0.5)).astype(BF16)
    ptr_load.wait()
    for out_load in out_loads:
        out_load.wait()

    peers = 1
    for d in range(1, reach + 1):
        peers = peers + (1 - (t + d) // frames) * (2 if d <= mem_reach else 1)
    pl.semaphore_wait(barrier, peers)

    part_copy = pltpu.make_async_remote_copy(
        src_ref=part,
        dst_ref=part_in,
        send_sem=near_send.at[0],
        recv_sem=near_recv.at[0],
        device_id=(t, other),
        device_id_type=MESH,
    )
    part_copy.start()
    halo_copy = pltpu.make_async_remote_copy(
        src_ref=joined.at[1 + other * (rows - 1)],
        dst_ref=halo,
        send_sem=near_send.at[1],
        recv_sem=near_recv.at[1],
        device_id=(t, other),
        device_id_type=MESH,
    )
    halo_copy.start()

    key_load.wait()
    value_load.wait()
    key_w = key_pad[mem_dim : 2 * mem_dim]
    value_w = value_pad[mem_dim : 2 * mem_dim]
    mem_tpos_keys = mm(mem_tpos[...], key_w)

    def cut(pointer_rows):
        return jnp.concatenate(
            [pointer_rows[:, j * mem_dim : (j + 1) * mem_dim] for j in range(parts)], axis=0
        )

    ptr_tokens = parts * POINTERS
    ptr_tpos_keys = mm(cut(ptr_tpos[...]), key_w)
    null_rows = jnp.broadcast_to(
        empty_memory[...].astype(F32).reshape(1, mem_dim), (ptr_tokens, mem_dim)
    ).astype(BF16)
    null_keys = mm(null_rows, key_w).astype(BF16)
    null_values = mm(null_rows, value_w).astype(BF16)

    part_copy.wait()
    pooled = part[...] + part_in[...]
    pooled = jnp.broadcast_to(pooled, (8, dim))
    normed = (
        pooled * lax.rsqrt(jnp.mean(pooled * pooled, axis=1, keepdims=True) + 1e-06)
    ).astype(BF16)
    pointer = mm(normed, ptrw[...]).astype(BF16)[0:1]
    ptr_send[0] = pointer.astype(F32)

    def ptr_copy(d):
        return pltpu.make_async_remote_copy(
            src_ref=ptr_send.at[0],
            dst_ref=ptr_in.at[d - 1],
            send_sem=ptr_send_sem.at[d - 1],
            recv_sem=ptr_recv_sem.at[d - 1],
            device_id=(t + d, s),
            device_id_type=MESH,
        )

    def mem_copy(d, to):
        return pltpu.make_async_remote_copy(
            src_ref=mem_send,
            dst_ref=mem_in.at[d - 1, s],
            send_sem=mem_send_sem.at[d - 1, to],
            recv_sem=mem_recv_sem.at[d - 1, s],
            device_id=(t + d, to),
            device_id_type=MESH,
        )

    for d in range(reach, 0, -1):

        @pl.when(t + d < frames)
        def _(d=d):
            ptr_copy(d).start()

    pointers[...] = pointer

    halo_copy.wait()
    tap = 2 * other
    edge = [mm(halo[...], taps[tap, b]) for b in range(3)]
    edge_rows = pl.ds(other * (tokens - columns), columns)
    conv[edge_rows] = conv[edge_rows] + shift_columns(*edge, col_of[0:columns])

    v = conv[...]
    hidden = (0.5 * v * (1.0 + jnp.tanh(0.7978845608 * (v + 0.044715 * (v * v * v))))).astype(BF16)
    twice = mm_t(hidden, outw[...])
    lane = lax.broadcasted_iota(jnp.int32, (half, 2 * mem_dim), 1)
    mem_send[...] = jnp.where(lane < mem_dim, twice[0:half], twice[half:tokens]).astype(BF16)
    for d in range(mem_reach, 0, -1):

        @pl.when(t + d < frames)
        def _(d=d):
            for to in range(2):
                mem_copy(d, to).start()

    mem_rows[...] = twice
    for c in range(0, columns, 2):
        even = mem_rows[pl.ds(c, rows, stride=columns), :]
        odd = mem_rows[pl.ds(c + 1, rows, stride=columns), :]
        memory[0, :, c * mem_dim : (c + 2) * mem_dim] = jnp.where(
            lane[0:rows] < mem_dim, even, odd
        ).astype(BF16)

    top = None
    key_low, key_high = key_pad[mem_dim : 3 * mem_dim], key_pad[0 : 2 * mem_dim]
    value_low, value_high = value_pad[mem_dim : 3 * mem_dim], value_pad[0 : 2 * mem_dim]
    column = 0

    def put(keys, vals, valid, at, top):
        count = keys.shape[0]
        block = jnp.where(valid, mm_t(query, keys), -jnp.inf)
        scores[:, at : at + count] = block
        values[at : at + count] = vals
        peak = jnp.max(block, axis=1, keepdims=True)
        return peak if top is None else jnp.maximum(top, peak)

    for d in range(1, MEMS + 1):
        for band in range(2):

            @pl.when(t - d >= 0)
            def _(d=d, band=band):
                pltpu.make_async_remote_copy(
                    src_ref=mem_send,
                    dst_ref=mem_in.at[d - 1, band],
                    send_sem=mem_send_sem.at[d - 1, band],
                    recv_sem=mem_recv_sem.at[d - 1, band],
                    device_id=(t, other),
                    device_id_type=MESH,
                ).wait_recv()

        packed = mem_in[d - 1].reshape(tokens, 2 * mem_dim)
        tpos = mem_tpos_keys[d - 1 : d]
        for key_half, value_half in ((key_low, value_low), (key_high, value_high)):
            keys = (mm(packed, key_half) + tpos).astype(BF16)
            vals = mm(packed, value_half).astype(BF16)
            top = put(keys, vals, t - d >= 0, column, top)
            column += tokens

    for d in range(1, reach + 1):

        @pl.when(t - d >= 0)
        def _(d=d):
            ptr_copy(d).wait_recv()

    tokens_in = cut(ptr_in[...].reshape(POINTERS, dim).astype(BF16))
    keys = jnp.concatenate(
        [(mm(tokens_in, key_w) + ptr_tpos_keys).astype(BF16), null_keys], axis=0
    )
    vals = jnp.concatenate([mm(tokens_in, value_w).astype(BF16), null_values], axis=0)
    index = lax.broadcasted_iota(jnp.int32, (1, 2 * ptr_tokens), 1)
    oldest = t - 1 - index % POINTERS
    valid = ((index < ptr_tokens) & (oldest >= 0)) | (index == ptr_tokens)
    top = put(keys, vals, valid, column, top)

    weights = jnp.exp(scores[...] - top)
    total = jnp.sum(weights, axis=1, keepdims=True)
    weights = (weights * (1.0 / total)).astype(BF16)
    mixed = mm(weights, values[...]).astype(BF16)
    proj_load.wait()
    result = feat[...].reshape(tokens, dim).astype(F32) + mm(mixed, projw[...])
    attended[0] = result.astype(BF16).reshape(rows, columns, dim)

    for d in range(1, reach + 1):

        @pl.when(t + d < frames)
        def _(d=d):
            ptr_copy(d).wait_send()
            if d <= mem_reach:
                for to in range(2):
                    mem_copy(d, to).wait_send()


def from_behind(block, axis, distance):
    devices = range(lax.axis_size(axis))
    route = [(i - distance, i) for i in devices if i - distance in devices]
    return lax.ppermute(block, axis, route)


def with_halo(block, sides, width):
    for axis, dim in sides:
        count = lax.axis_size(axis)
        forward = [(i, i + 1) for i in range(count - 1)]
        backward = [(target, source) for source, target in forward]
        low = lax.ppermute(
            lax.slice_in_dim(block, block.shape[dim] - width, None, axis=dim), axis, forward
        )
        high = lax.ppermute(lax.slice_in_dim(block, 0, width, axis=dim), axis, backward)
        block = jnp.concatenate([low, block, high], axis=dim)
    return block


def fetch_earlier(carried, hop_count):
    pieces = []
    for step_index in range(hop_count):
        pieces.append(from_behind(carried, "tm", step_index + 1))
    return jnp.concatenate(pieces[::-1], axis=0)


def attend(query, blocks):
    scores = []
    row_top = None
    for key_rows, value_rows, is_valid in blocks:
        block_scores = lax.dot_general(
            query, key_rows, (((1,), (1,)), ((), ())), preferred_element_type=jnp.float32
        )
        block_scores = jnp.where(is_valid, block_scores, -jnp.inf)
        scores.append(block_scores)
        block_top = jnp.max(block_scores, axis=1, keepdims=True)
        row_top = block_top if row_top is None else jnp.maximum(row_top, block_top)
    row_total = jnp.zeros_like(row_top)
    for block_scores in scores:
        row_total = row_total + jnp.sum(jnp.exp(block_scores - row_top), axis=1, keepdims=True)
    mixed_sum = jnp.zeros((query.shape[0], blocks[0][1].shape[1]), jnp.float32)
    for block_scores, block in zip(scores, blocks):
        weights = (jnp.exp(block_scores - row_top) / row_total).astype(jnp.bfloat16)
        mixed_sum = mixed_sum + jnp.dot(weights, block[1], preferred_element_type=jnp.float32)
    return mixed_sum.astype(jnp.bfloat16)


def staged_body(
    features,
    masks,
    w_pix,
    mask_embed,
    w_conv,
    w_out,
    w_ptr,
    w_query,
    w_key,
    w_value,
    w_proj,
    mem_tpos,
    ptr_tpos,
    empty_memory,
):
    frames_dev, rows_dev, columns, model_dim = features.shape
    mem_dim = w_key.shape[0]
    ptr_tok = model_dim // mem_dim
    band_tokens = rows_dev * columns
    flat_rows = features.reshape(frames_dev * band_tokens, model_dim)
    mask_rows = masks.reshape(frames_dev * band_tokens, 1).astype(jnp.float32)
    joined_map = (
        jnp.dot(flat_rows, w_pix, preferred_element_type=jnp.float32)
        + mask_rows * mask_embed.astype(jnp.float32)
    ).astype(jnp.bfloat16)
    joined_map = joined_map.reshape(frames_dev, rows_dev, columns, model_dim)
    padded = with_halo(joined_map, (("space", 1),), 1)
    padded = jnp.pad(padded, ((0, 0), (0, 0), (1, 1), (0, 0)))
    conv_sum = jnp.zeros((frames_dev * band_tokens, model_dim), jnp.float32)
    for row_tap in range(3):
        for col_tap in range(3):
            window_rows = padded[
                :, row_tap : row_tap + rows_dev, col_tap : col_tap + columns, :
            ].reshape(-1, model_dim)
            conv_sum = conv_sum + jnp.dot(
                window_rows, w_conv[row_tap, col_tap], preferred_element_type=jnp.float32
            )
    hidden = jax.nn.gelu(conv_sum, approximate=True).astype(jnp.bfloat16)
    memory = jnp.dot(hidden, w_out, preferred_element_type=jnp.float32).astype(jnp.bfloat16)
    memory = memory.reshape(frames_dev, rows_dev, columns * mem_dim)
    band_mask = masks.reshape(frames_dev, band_tokens).astype(jnp.bfloat16)
    partial_value = jnp.einsum(
        "ft,ftd->fd",
        band_mask,
        features.reshape(frames_dev, band_tokens, model_dim),
        preferred_element_type=jnp.float32,
    )
    pooled = lax.psum(partial_value, "space")
    normed = (pooled * lax.rsqrt(jnp.mean(pooled * pooled, axis=1, keepdims=True) + 1e-06)).astype(
        jnp.bfloat16
    )
    pointers = jnp.dot(normed, w_ptr, preferred_element_type=jnp.float32).astype(jnp.bfloat16)
    all_pointers = lax.all_gather(pointers, "tm", axis=0, tiled=True)
    hop_count = (MEMS + frames_dev - 1) // frames_dev
    carried = lax.all_gather(memory, "space", axis=1, tiled=True)
    history = jnp.concatenate(
        [fetch_earlier(carried, hop_count), carried[: frames_dev - 1]], axis=0
    )
    grid_tokens = columns * columns
    hist_frames = history.shape[0]
    history = history.reshape(hist_frames, grid_tokens, mem_dim)
    hist_values = jnp.dot(
        history.reshape(-1, mem_dim), w_value, preferred_element_type=jnp.float32
    ).astype(jnp.bfloat16)
    hist_values = hist_values.reshape(hist_frames, grid_tokens, model_dim)
    tpos_keys = jnp.dot(mem_tpos, w_key, preferred_element_type=jnp.float32)
    ptr_tpos_keys = jnp.dot(
        ptr_tpos[::-1].reshape(POINTERS * ptr_tok, mem_dim),
        w_key,
        preferred_element_type=jnp.float32,
    )
    null_key = jnp.dot(
        empty_memory.reshape(1, mem_dim), w_key, preferred_element_type=jnp.float32
    ).astype(jnp.bfloat16)
    null_value = jnp.dot(
        empty_memory.reshape(1, mem_dim), w_value, preferred_element_type=jnp.float32
    ).astype(jnp.bfloat16)
    padded_ptr = jnp.concatenate(
        [jnp.zeros((POINTERS, model_dim), jnp.bfloat16), all_pointers], axis=0
    )
    ptr_offsets = jnp.repeat(jnp.arange(POINTERS, dtype=jnp.int32) - POINTERS, ptr_tok)
    features_f = features.reshape(frames_dev, band_tokens, model_dim).astype(jnp.float32)
    first_frame = lax.axis_index("tm") * frames_dev
    frame = first_frame + 0
    rows_f = features_f[0]
    centred = rows_f - jnp.mean(rows_f, axis=1, keepdims=True)
    query_in = (
        centred * lax.rsqrt(jnp.mean(centred * centred, axis=1, keepdims=True) + 1e-05)
    ).astype(jnp.bfloat16)
    query = (
        jnp.dot(query_in, w_query, preferred_element_type=jnp.float32) * model_dim ** (-0.5)
    ).astype(jnp.bfloat16)
    blocks = []
    for distance in range(1, MEMS + 1):
        slot_index = hop_count * frames_dev - distance
        key_rows = (
            jnp.dot(history[slot_index], w_key, preferred_element_type=jnp.float32)
            + tpos_keys[distance - 1]
        ).astype(jnp.bfloat16)
        blocks.append((key_rows, hist_values[slot_index], frame - distance >= 0))
    window = lax.dynamic_slice_in_dim(padded_ptr, frame, POINTERS, 0)
    ptr_tokens = window.reshape(POINTERS * ptr_tok, mem_dim)
    ptr_keys = (
        jnp.dot(ptr_tokens, w_key, preferred_element_type=jnp.float32) + ptr_tpos_keys
    ).astype(jnp.bfloat16)
    ptr_values = jnp.dot(ptr_tokens, w_value, preferred_element_type=jnp.float32).astype(
        jnp.bfloat16
    )
    extra_valid = jnp.concatenate([frame + ptr_offsets >= 0, jnp.ones((1,), bool)], axis=0)
    blocks.append(
        (
            jnp.concatenate([ptr_keys, null_key], axis=0),
            jnp.concatenate([ptr_values, null_value], axis=0),
            extra_valid[None, :],
        )
    )
    mixed_rows = attend(query, blocks)
    outputs = [
        (rows_f + jnp.dot(mixed_rows, w_proj, preferred_element_type=jnp.float32)).astype(
            jnp.bfloat16
        )
    ]
    attended = jnp.stack(outputs, axis=0).reshape(frames_dev, rows_dev, columns, model_dim)
    return (attended, memory, pointers)


def fused_body(
    features,
    masks,
    w_pix,
    mask_embed,
    w_conv,
    w_out,
    w_ptr,
    w_query,
    w_key,
    w_value,
    w_proj,
    mem_tpos,
    ptr_tpos,
    empty_memory,
):
    _, rows, columns, dim = features.shape
    frames = lax.axis_size("tm")
    mem_dim = w_key.shape[0]
    tokens = rows * columns
    half = tokens // 2
    key_count = MEMS * 2 * tokens + 2 * POINTERS * (dim // mem_dim)
    vmem = pl.BlockSpec(memory_space=pltpu.VMEM)
    hbm = pl.BlockSpec(memory_space=pl.ANY)
    dma = pltpu.SemaphoreType.DMA
    return pl.pallas_call(
        functools.partial(kernel, frames),
        out_shape=(
            jax.ShapeDtypeStruct(features.shape, BF16),
            jax.ShapeDtypeStruct((1, rows, columns * mem_dim), BF16),
            jax.ShapeDtypeStruct((1, dim), BF16),
        ),
        in_specs=[hbm] + [vmem] * 5 + [hbm] * 8,
        out_specs=(vmem, vmem, vmem),
        scratch_shapes=[
            pltpu.VMEM((rows, columns, dim), BF16),
            pltpu.VMEM(w_pix.shape, BF16),
            pltpu.VMEM(w_conv.shape, BF16),
            pltpu.VMEM((2 * mem_dim, dim), BF16),
            pltpu.VMEM(w_ptr.shape, BF16),
            pltpu.VMEM(w_query.shape, BF16),
            pltpu.VMEM((3 * mem_dim, dim), BF16),
            pltpu.VMEM((3 * mem_dim, dim), BF16),
            pltpu.VMEM(w_proj.shape, BF16),
            pltpu.VMEM((rows + 2, columns, dim), BF16),
            pltpu.VMEM((columns, dim), BF16),
            pltpu.VMEM((tokens, dim), F32),
            pltpu.VMEM((1, dim), F32),
            pltpu.VMEM((1, dim), F32),
            pltpu.VMEM((tokens, 2 * mem_dim), F32),
            pltpu.VMEM((half, 2 * mem_dim), BF16),
            pltpu.VMEM((MEMS, 2, half, 2 * mem_dim), BF16),
            pltpu.VMEM((1, 1, dim), F32),
            pltpu.VMEM((POINTERS, 1, dim), F32),
            pltpu.VMEM((tokens, key_count), F32),
            pltpu.VMEM((key_count, dim), BF16),
            dma((12,)),
            dma((2,)),
            dma((2,)),
            dma((MEMS, 2)),
            dma((MEMS, 2)),
            dma((POINTERS,)),
            dma((POINTERS,)),
        ],
        compiler_params=pltpu.CompilerParams(collective_id=0, has_side_effects=True),
    )(
        features,
        masks,
        mask_embed,
        mem_tpos,
        ptr_tpos,
        empty_memory,
        w_pix,
        w_conv,
        w_out.T,
        w_ptr,
        w_query,
        w_key,
        w_value,
        w_proj,
    )


def body(features, *rest):
    frames_dev, rows, columns, dim = features.shape
    key_count = MEMS * 2 * rows * columns
    fits = rows * columns * key_count * 4 <= 2**23 and rows * columns <= 256
    if frames_dev == 1 and lax.axis_size("space") == 2 and fits:
        return fused_body(features, *rest)
    return staged_body(features, *rest)


def solution(mesh):
    return jax.shard_map(
        body,
        mesh=mesh,
        in_specs=(P("tm", "space", None, None), P("tm", "space", None)) + (P(),) * 12,
        out_specs=(P("tm", "space", None, None), P("tm", "space", None), P("tm", None)),
        check_vma=False,
    )
```

```python
import functools

import jax
import jax.numpy as jnp
from jax import lax
from jax.experimental import pallas as pl
from jax.experimental.pallas import tpu as pltpu
from jax.sharding import PartitionSpec as P

MEMS = 3
POINTERS = 16
MESH = pl.DeviceIdType.MESH
F32 = jnp.float32
BF16 = jnp.bfloat16


def mm(a, b):
    return jnp.dot(a, b, preferred_element_type=F32)


def mm_t(a, b):
    return lax.dot_general(a, b, (((1,), (1,)), ((), ())), preferred_element_type=F32)


def kernel(
    frames,
    features,
    masks_in,
    mask_embed_in,
    mem_tpos_in,
    ptr_tpos_in,
    empty_memory_in,
    w_pix,
    w_conv,
    w_out_t,
    w_ptr,
    w_query,
    w_key,
    w_value,
    w_proj,
    attended,
    memory,
    pointers,
    feat,
    masks,
    mask_embed,
    mem_tpos,
    ptr_tpos,
    empty_memory,
    pix,
    taps,
    outw,
    ptrw,
    queryw,
    key_pad,
    value_pad,
    projw,
    joined,
    halo,
    conv,
    part,
    part_in,
    mem_rows,
    mem_send,
    mem_in,
    ptr_send,
    ptr_in,
    scores,
    values,
    load_sem,
    near_send,
    near_recv,
    mem_send_sem,
    mem_recv_sem,
    ptr_send_sem,
    ptr_recv_sem,
):
    _, rows, columns, dim = features.shape
    tokens = rows * columns
    mem_dim = w_key.shape[0]
    half = tokens // 2
    parts = dim // mem_dim
    t = lax.axis_index("tm")
    s = lax.axis_index("space")
    other = 1 - s
    reach = min(POINTERS, frames - 1)
    mem_reach = min(MEMS, frames - 1)

    barrier = pltpu.get_barrier_semaphore()
    pl.semaphore_signal(barrier, inc=1, device_id=(t, other), device_id_type=MESH)
    for d in range(reach, 0, -1):

        @pl.when(t - d >= 0)
        def _(d=d):
            pl.semaphore_signal(barrier, inc=1, device_id=(t - d, s), device_id_type=MESH)
            if d <= mem_reach:
                pl.semaphore_signal(
                    barrier, inc=1, device_id=(t - d, other), device_id_type=MESH
                )

    loads = []

    def load(src, dst):
        copy = pltpu.make_async_copy(src, dst, load_sem.at[len(loads)])
        copy.start()
        loads.append(copy)
        return copy

    feat_load = load(features.at[0], feat)
    mask_load = load(masks_in, masks)
    embed_load = load(mask_embed_in, mask_embed)
    pix_load = load(w_pix, pix)
    tap_loads = [load(w_conv.at[a], taps.at[a]) for a in range(3)]
    query_load = load(w_query, queryw)
    ptr_load = load(w_ptr, ptrw)
    out_loads = [load(w_out_t, outw.at[pl.ds(k * mem_dim, mem_dim)]) for k in range(2)]
    key_load = load(w_key, key_pad.at[pl.ds(mem_dim, mem_dim)])
    value_load = load(w_value, value_pad.at[pl.ds(mem_dim, mem_dim)])
    small_loads = [
        load(mem_tpos_in, mem_tpos),
        load(ptr_tpos_in, ptr_tpos),
        load(empty_memory_in, empty_memory),
    ]
    proj_load = load(w_proj, projw)

    blank = jnp.zeros((mem_dim, dim), BF16)
    for ref in (key_pad, value_pad):
        ref[0:mem_dim] = blank
        ref[2 * mem_dim : 3 * mem_dim] = blank
    joined[0] = jnp.zeros((columns, dim), BF16)
    joined[rows + 1] = jnp.zeros((columns, dim), BF16)
    for d in range(1, MEMS + 1):

        @pl.when(t - d < 0)
        def _(d=d):
            mem_in[d - 1] = jnp.zeros((2, half, 2 * mem_dim), BF16)

    for d in range(1, POINTERS + 1):

        @pl.when(t - d < 0)
        def _(d=d):
            ptr_in[d - 1] = jnp.zeros((1, dim), F32)

    mask_load.wait()
    mask_f = masks[0].astype(F32)
    spread = jnp.concatenate(
        [jnp.broadcast_to(mask_f[r : r + 1], (columns, columns)) for r in range(rows)], axis=0
    )
    token_col = lax.broadcasted_iota(jnp.int32, (tokens, columns), 0) % columns
    lane_col = lax.broadcasted_iota(jnp.int32, (tokens, columns), 1)
    mask_col = jnp.sum(jnp.where(token_col == lane_col, spread, 0.0), axis=1, keepdims=True)
    col_of = lax.broadcasted_iota(jnp.int32, (tokens, dim), 0) % columns

    feat_load.wait()
    flat = feat[...].reshape(tokens, dim)
    flat_f = flat.astype(F32)
    part[...] = jnp.sum(mask_col * flat_f, axis=0, keepdims=True)
    pix_load.wait()
    embed_load.wait()
    joined_rows = (
        mm(flat, pix[...]) + mask_col * mask_embed[...].astype(F32).reshape(1, dim)
    ).astype(BF16)
    joined[1 : rows + 1] = joined_rows.reshape(rows, columns, dim)

    sums = [None, None, None]
    for a in range(3):
        tap_loads[a].wait()
        window = joined[a : a + rows].reshape(tokens, dim)
        for b in range(3):
            product = mm(window, taps[a, b])
            sums[b] = product if sums[b] is None else sums[b] + product

    def shift_columns(low, mid, high, col):
        count = low.shape[0]
        low = jnp.where(col == 0, 0.0, pltpu.roll(low, 1, 0))
        high = jnp.where(col == columns - 1, 0.0, pltpu.roll(high, count - 1, 0))
        return mid + low + high

    conv[...] = shift_columns(*sums, col_of)

    centred = flat_f - jnp.mean(flat_f, axis=1, keepdims=True)
    query_in = (
        centred * lax.rsqrt(jnp.mean(centred * centred, axis=1, keepdims=True) + 1e-05)
    ).astype(BF16)
    query_load.wait()
    query = (mm(query_in, queryw[...]) * dim ** (-0.5)).astype(BF16)
    ptr_load.wait()
    for out_load in out_loads:
        out_load.wait()

    peers = 1
    for d in range(1, reach + 1):
        peers = peers + (1 - (t + d) // frames) * (2 if d <= mem_reach else 1)
    pl.semaphore_wait(barrier, peers)

    part_copy = pltpu.make_async_remote_copy(
        src_ref=part,
        dst_ref=part_in,
        send_sem=near_send.at[0],
        recv_sem=near_recv.at[0],
        device_id=(t, other),
        device_id_type=MESH,
    )
    part_copy.start()
    halo_copy = pltpu.make_async_remote_copy(
        src_ref=joined.at[1 + other * (rows - 1)],
        dst_ref=halo,
        send_sem=near_send.at[1],
        recv_sem=near_recv.at[1],
        device_id=(t, other),
        device_id_type=MESH,
    )
    halo_copy.start()

    key_load.wait()
    value_load.wait()
    for small_load in small_loads:
        small_load.wait()
    key_w = key_pad[mem_dim : 2 * mem_dim]
    value_w = value_pad[mem_dim : 2 * mem_dim]
    mem_tpos_keys = mm(mem_tpos[...], key_w)

    def cut(pointer_rows):
        return jnp.concatenate(
            [pointer_rows[:, j * mem_dim : (j + 1) * mem_dim] for j in range(parts)], axis=0
        )

    ptr_tokens = parts * POINTERS
    ptr_tpos_keys = mm(cut(ptr_tpos[...]), key_w)
    null_rows = jnp.broadcast_to(
        empty_memory[...].astype(F32).reshape(1, mem_dim), (ptr_tokens, mem_dim)
    ).astype(BF16)
    null_keys = mm(null_rows, key_w).astype(BF16)
    null_values = mm(null_rows, value_w).astype(BF16)

    part_copy.wait()
    pooled = part[...] + part_in[...]
    pooled = jnp.broadcast_to(pooled, (8, dim))
    normed = (
        pooled * lax.rsqrt(jnp.mean(pooled * pooled, axis=1, keepdims=True) + 1e-06)
    ).astype(BF16)
    pointer = mm(normed, ptrw[...]).astype(BF16)[0:1]
    ptr_send[0] = pointer.astype(F32)

    def ptr_copy(d):
        return pltpu.make_async_remote_copy(
            src_ref=ptr_send.at[0],
            dst_ref=ptr_in.at[d - 1],
            send_sem=ptr_send_sem.at[d - 1],
            recv_sem=ptr_recv_sem.at[d - 1],
            device_id=(t + d, s),
            device_id_type=MESH,
        )

    def mem_copy(d, to):
        return pltpu.make_async_remote_copy(
            src_ref=mem_send,
            dst_ref=mem_in.at[d - 1, s],
            send_sem=mem_send_sem.at[d - 1, to],
            recv_sem=mem_recv_sem.at[d - 1, s],
            device_id=(t + d, to),
            device_id_type=MESH,
        )

    for d in range(reach, 0, -1):

        @pl.when(t + d < frames)
        def _(d=d):
            ptr_copy(d).start()

    pointers[...] = pointer

    halo_copy.wait()
    tap = 2 * other
    edge = [mm(halo[...], taps[tap, b]) for b in range(3)]
    edge_rows = pl.ds(other * (tokens - columns), columns)
    conv[edge_rows] = conv[edge_rows] + shift_columns(*edge, col_of[0:columns])

    v = conv[...]
    hidden = (0.5 * v * (1.0 + jnp.tanh(0.7978845608 * (v + 0.044715 * (v * v * v))))).astype(BF16)
    twice = mm_t(hidden, outw[...])
    lane = lax.broadcasted_iota(jnp.int32, (half, 2 * mem_dim), 1)
    mem_send[...] = jnp.where(lane < mem_dim, twice[0:half], twice[half:tokens]).astype(BF16)
    for d in range(mem_reach, 0, -1):

        @pl.when(t + d < frames)
        def _(d=d):
            for to in range(2):
                mem_copy(d, to).start()

    mem_rows[...] = twice
    for c in range(0, columns, 2):
        even = mem_rows[pl.ds(c, rows, stride=columns), :]
        odd = mem_rows[pl.ds(c + 1, rows, stride=columns), :]
        memory[0, :, c * mem_dim : (c + 2) * mem_dim] = jnp.where(
            lane[0:rows] < mem_dim, even, odd
        ).astype(BF16)

    top = None
    key_low, key_high = key_pad[mem_dim : 3 * mem_dim], key_pad[0 : 2 * mem_dim]
    value_low, value_high = value_pad[mem_dim : 3 * mem_dim], value_pad[0 : 2 * mem_dim]
    column = 0

    def put(keys, vals, valid, at, top):
        count = keys.shape[0]
        block = jnp.where(valid, mm_t(query, keys), -jnp.inf)
        scores[:, at : at + count] = block
        values[at : at + count] = vals
        peak = jnp.max(block, axis=1, keepdims=True)
        return peak if top is None else jnp.maximum(top, peak)

    for d in range(1, MEMS + 1):
        for band in range(2):

            @pl.when(t - d >= 0)
            def _(d=d, band=band):
                pltpu.make_async_remote_copy(
                    src_ref=mem_send,
                    dst_ref=mem_in.at[d - 1, band],
                    send_sem=mem_send_sem.at[d - 1, band],
                    recv_sem=mem_recv_sem.at[d - 1, band],
                    device_id=(t, other),
                    device_id_type=MESH,
                ).wait_recv()

        packed = mem_in[d - 1].reshape(tokens, 2 * mem_dim)
        tpos = mem_tpos_keys[d - 1 : d]
        for key_half, value_half in ((key_low, value_low), (key_high, value_high)):
            keys = (mm(packed, key_half) + tpos).astype(BF16)
            vals = mm(packed, value_half).astype(BF16)
            top = put(keys, vals, t - d >= 0, column, top)
            column += tokens

    for d in range(1, reach + 1):

        @pl.when(t - d >= 0)
        def _(d=d):
            ptr_copy(d).wait_recv()

    tokens_in = cut(ptr_in[...].reshape(POINTERS, dim).astype(BF16))
    keys = jnp.concatenate(
        [(mm(tokens_in, key_w) + ptr_tpos_keys).astype(BF16), null_keys], axis=0
    )
    vals = jnp.concatenate([mm(tokens_in, value_w).astype(BF16), null_values], axis=0)
    index = lax.broadcasted_iota(jnp.int32, (1, 2 * ptr_tokens), 1)
    oldest = t - 1 - index % POINTERS
    valid = ((index < ptr_tokens) & (oldest >= 0)) | (index == ptr_tokens)
    top = put(keys, vals, valid, column, top)

    weights = jnp.exp(scores[...] - top)
    total = jnp.sum(weights, axis=1, keepdims=True)
    weights = (weights * (1.0 / total)).astype(BF16)
    mixed = mm(weights, values[...]).astype(BF16)
    proj_load.wait()
    result = feat[...].reshape(tokens, dim).astype(F32) + mm(mixed, projw[...])
    attended[0] = result.astype(BF16).reshape(rows, columns, dim)

    for d in range(1, reach + 1):

        @pl.when(t + d < frames)
        def _(d=d):
            ptr_copy(d).wait_send()
            if d <= mem_reach:
                for to in range(2):
                    mem_copy(d, to).wait_send()


def from_behind(block, axis, distance):
    devices = range(lax.axis_size(axis))
    route = [(i - distance, i) for i in devices if i - distance in devices]
    return lax.ppermute(block, axis, route)


def with_halo(block, sides, width):
    for axis, dim in sides:
        count = lax.axis_size(axis)
        forward = [(i, i + 1) for i in range(count - 1)]
        backward = [(target, source) for source, target in forward]
        low = lax.ppermute(
            lax.slice_in_dim(block, block.shape[dim] - width, None, axis=dim), axis, forward
        )
        high = lax.ppermute(lax.slice_in_dim(block, 0, width, axis=dim), axis, backward)
        block = jnp.concatenate([low, block, high], axis=dim)
    return block


def fetch_earlier(carried, hop_count):
    pieces = []
    for step_index in range(hop_count):
        pieces.append(from_behind(carried, "tm", step_index + 1))
    return jnp.concatenate(pieces[::-1], axis=0)


def attend(query, blocks):
    scores = []
    row_top = None
    for key_rows, value_rows, is_valid in blocks:
        block_scores = lax.dot_general(
            query, key_rows, (((1,), (1,)), ((), ())), preferred_element_type=jnp.float32
        )
        block_scores = jnp.where(is_valid, block_scores, -jnp.inf)
        scores.append(block_scores)
        block_top = jnp.max(block_scores, axis=1, keepdims=True)
        row_top = block_top if row_top is None else jnp.maximum(row_top, block_top)
    row_total = jnp.zeros_like(row_top)
    for block_scores in scores:
        row_total = row_total + jnp.sum(jnp.exp(block_scores - row_top), axis=1, keepdims=True)
    mixed_sum = jnp.zeros((query.shape[0], blocks[0][1].shape[1]), jnp.float32)
    for block_scores, block in zip(scores, blocks):
        weights = (jnp.exp(block_scores - row_top) / row_total).astype(jnp.bfloat16)
        mixed_sum = mixed_sum + jnp.dot(weights, block[1], preferred_element_type=jnp.float32)
    return mixed_sum.astype(jnp.bfloat16)


def staged_body(
    features,
    masks,
    w_pix,
    mask_embed,
    w_conv,
    w_out,
    w_ptr,
    w_query,
    w_key,
    w_value,
    w_proj,
    mem_tpos,
    ptr_tpos,
    empty_memory,
):
    frames_dev, rows_dev, columns, model_dim = features.shape
    mem_dim = w_key.shape[0]
    ptr_tok = model_dim // mem_dim
    band_tokens = rows_dev * columns
    flat_rows = features.reshape(frames_dev * band_tokens, model_dim)
    mask_rows = masks.reshape(frames_dev * band_tokens, 1).astype(jnp.float32)
    joined_map = (
        jnp.dot(flat_rows, w_pix, preferred_element_type=jnp.float32)
        + mask_rows * mask_embed.astype(jnp.float32)
    ).astype(jnp.bfloat16)
    joined_map = joined_map.reshape(frames_dev, rows_dev, columns, model_dim)
    padded = with_halo(joined_map, (("space", 1),), 1)
    padded = jnp.pad(padded, ((0, 0), (0, 0), (1, 1), (0, 0)))
    conv_sum = jnp.zeros((frames_dev * band_tokens, model_dim), jnp.float32)
    for row_tap in range(3):
        for col_tap in range(3):
            window_rows = padded[
                :, row_tap : row_tap + rows_dev, col_tap : col_tap + columns, :
            ].reshape(-1, model_dim)
            conv_sum = conv_sum + jnp.dot(
                window_rows, w_conv[row_tap, col_tap], preferred_element_type=jnp.float32
            )
    hidden = jax.nn.gelu(conv_sum, approximate=True).astype(jnp.bfloat16)
    memory = jnp.dot(hidden, w_out, preferred_element_type=jnp.float32).astype(jnp.bfloat16)
    memory = memory.reshape(frames_dev, rows_dev, columns * mem_dim)
    band_mask = masks.reshape(frames_dev, band_tokens).astype(jnp.bfloat16)
    partial_value = jnp.einsum(
        "ft,ftd->fd",
        band_mask,
        features.reshape(frames_dev, band_tokens, model_dim),
        preferred_element_type=jnp.float32,
    )
    pooled = lax.psum(partial_value, "space")
    normed = (pooled * lax.rsqrt(jnp.mean(pooled * pooled, axis=1, keepdims=True) + 1e-06)).astype(
        jnp.bfloat16
    )
    pointers = jnp.dot(normed, w_ptr, preferred_element_type=jnp.float32).astype(jnp.bfloat16)
    all_pointers = lax.all_gather(pointers, "tm", axis=0, tiled=True)
    hop_count = (MEMS + frames_dev - 1) // frames_dev
    carried = lax.all_gather(memory, "space", axis=1, tiled=True)
    history = jnp.concatenate(
        [fetch_earlier(carried, hop_count), carried[: frames_dev - 1]], axis=0
    )
    grid_tokens = columns * columns
    hist_frames = history.shape[0]
    history = history.reshape(hist_frames, grid_tokens, mem_dim)
    hist_values = jnp.dot(
        history.reshape(-1, mem_dim), w_value, preferred_element_type=jnp.float32
    ).astype(jnp.bfloat16)
    hist_values = hist_values.reshape(hist_frames, grid_tokens, model_dim)
    tpos_keys = jnp.dot(mem_tpos, w_key, preferred_element_type=jnp.float32)
    ptr_tpos_keys = jnp.dot(
        ptr_tpos[::-1].reshape(POINTERS * ptr_tok, mem_dim),
        w_key,
        preferred_element_type=jnp.float32,
    )
    null_key = jnp.dot(
        empty_memory.reshape(1, mem_dim), w_key, preferred_element_type=jnp.float32
    ).astype(jnp.bfloat16)
    null_value = jnp.dot(
        empty_memory.reshape(1, mem_dim), w_value, preferred_element_type=jnp.float32
    ).astype(jnp.bfloat16)
    padded_ptr = jnp.concatenate(
        [jnp.zeros((POINTERS, model_dim), jnp.bfloat16), all_pointers], axis=0
    )
    ptr_offsets = jnp.repeat(jnp.arange(POINTERS, dtype=jnp.int32) - POINTERS, ptr_tok)
    features_f = features.reshape(frames_dev, band_tokens, model_dim).astype(jnp.float32)
    first_frame = lax.axis_index("tm") * frames_dev
    frame = first_frame + 0
    rows_f = features_f[0]
    centred = rows_f - jnp.mean(rows_f, axis=1, keepdims=True)
    query_in = (
        centred * lax.rsqrt(jnp.mean(centred * centred, axis=1, keepdims=True) + 1e-05)
    ).astype(jnp.bfloat16)
    query = (
        jnp.dot(query_in, w_query, preferred_element_type=jnp.float32) * model_dim ** (-0.5)
    ).astype(jnp.bfloat16)
    blocks = []
    for distance in range(1, MEMS + 1):
        slot_index = hop_count * frames_dev - distance
        key_rows = (
            jnp.dot(history[slot_index], w_key, preferred_element_type=jnp.float32)
            + tpos_keys[distance - 1]
        ).astype(jnp.bfloat16)
        blocks.append((key_rows, hist_values[slot_index], frame - distance >= 0))
    window = lax.dynamic_slice_in_dim(padded_ptr, frame, POINTERS, 0)
    ptr_tokens = window.reshape(POINTERS * ptr_tok, mem_dim)
    ptr_keys = (
        jnp.dot(ptr_tokens, w_key, preferred_element_type=jnp.float32) + ptr_tpos_keys
    ).astype(jnp.bfloat16)
    ptr_values = jnp.dot(ptr_tokens, w_value, preferred_element_type=jnp.float32).astype(
        jnp.bfloat16
    )
    extra_valid = jnp.concatenate([frame + ptr_offsets >= 0, jnp.ones((1,), bool)], axis=0)
    blocks.append(
        (
            jnp.concatenate([ptr_keys, null_key], axis=0),
            jnp.concatenate([ptr_values, null_value], axis=0),
            extra_valid[None, :],
        )
    )
    mixed_rows = attend(query, blocks)
    outputs = [
        (rows_f + jnp.dot(mixed_rows, w_proj, preferred_element_type=jnp.float32)).astype(
            jnp.bfloat16
        )
    ]
    attended = jnp.stack(outputs, axis=0).reshape(frames_dev, rows_dev, columns, model_dim)
    return (attended, memory, pointers)


def put_out(*refs):
    sem = refs[-1]
    copies = [pltpu.make_async_copy(refs[k], refs[3 + k], sem.at[k]) for k in range(3)]
    for copy in copies:
        copy.start()
    for copy in copies:
        copy.wait()


def fused_body(
    features,
    masks,
    w_pix,
    mask_embed,
    w_conv,
    w_out,
    w_ptr,
    w_query,
    w_key,
    w_value,
    w_proj,
    mem_tpos,
    ptr_tpos,
    empty_memory,
):
    _, rows, columns, dim = features.shape
    frames = lax.axis_size("tm")
    mem_dim = w_key.shape[0]
    tokens = rows * columns
    half = tokens // 2
    key_count = MEMS * 2 * tokens + 2 * POINTERS * (dim // mem_dim)
    vmem = pl.BlockSpec(memory_space=pltpu.VMEM)
    hbm = pl.BlockSpec(memory_space=pltpu.HBM)
    dma = pltpu.SemaphoreType.DMA
    results = pl.pallas_call(
        functools.partial(kernel, frames),
        out_shape=(
            pltpu.VMEM(features.shape, BF16),
            pltpu.VMEM((1, rows, columns * mem_dim), BF16),
            pltpu.VMEM((1, dim), BF16),
        ),
        in_specs=[hbm] * 14,
        out_specs=(vmem, vmem, vmem),
        scratch_shapes=[
            pltpu.VMEM((rows, columns, dim), BF16),
            pltpu.VMEM(masks.shape, masks.dtype),
            pltpu.VMEM(mask_embed.shape, BF16),
            pltpu.VMEM(mem_tpos.shape, BF16),
            pltpu.VMEM(ptr_tpos.shape, BF16),
            pltpu.VMEM(empty_memory.shape, BF16),
            pltpu.VMEM(w_pix.shape, BF16),
            pltpu.VMEM(w_conv.shape, BF16),
            pltpu.VMEM((2 * mem_dim, dim), BF16),
            pltpu.VMEM(w_ptr.shape, BF16),
            pltpu.VMEM(w_query.shape, BF16),
            pltpu.VMEM((3 * mem_dim, dim), BF16),
            pltpu.VMEM((3 * mem_dim, dim), BF16),
            pltpu.VMEM(w_proj.shape, BF16),
            pltpu.VMEM((rows + 2, columns, dim), BF16),
            pltpu.VMEM((columns, dim), BF16),
            pltpu.VMEM((tokens, dim), F32),
            pltpu.VMEM((1, dim), F32),
            pltpu.VMEM((1, dim), F32),
            pltpu.VMEM((tokens, 2 * mem_dim), F32),
            pltpu.VMEM((half, 2 * mem_dim), BF16),
            pltpu.VMEM((MEMS, 2, half, 2 * mem_dim), BF16),
            pltpu.VMEM((1, 1, dim), F32),
            pltpu.VMEM((POINTERS, 1, dim), F32),
            pltpu.VMEM((tokens, key_count), F32),
            pltpu.VMEM((key_count, dim), BF16),
            dma((17,)),
            dma((2,)),
            dma((2,)),
            dma((MEMS, 2)),
            dma((MEMS, 2)),
            dma((POINTERS,)),
            dma((POINTERS,)),
        ],
        compiler_params=pltpu.CompilerParams(
            collective_id=0, has_side_effects=True
        ),
    )(
        features,
        masks,
        mask_embed,
        mem_tpos,
        ptr_tpos,
        empty_memory,
        w_pix,
        w_conv,
        w_out.T,
        w_ptr,
        w_query,
        w_key,
        w_value,
        w_proj,
    )
    return pl.pallas_call(
        put_out,
        out_shape=tuple(jax.ShapeDtypeStruct(x.shape, x.dtype) for x in results),
        in_specs=[vmem] * 3,
        out_specs=(hbm,) * 3,
        scratch_shapes=[dma((3,))],
        compiler_params=pltpu.CompilerParams(vmem_limit_bytes=2**20),
    )(*[pltpu.with_memory_space_constraint(x, pltpu.VMEM) for x in results])


def body(features, *rest):
    frames_dev, rows, columns, dim = features.shape
    key_count = MEMS * 2 * rows * columns
    fits = rows * columns * key_count * 4 <= 2**23 and rows * columns <= 256
    if frames_dev == 1 and lax.axis_size("space") == 2 and fits:
        return fused_body(features, *rest)
    return staged_body(features, *rest)


def solution(mesh):
    return jax.shard_map(
        body,
        mesh=mesh,
        in_specs=(P("tm", "space", None, None), P("tm", "space", None)) + (P(),) * 12,
        out_specs=(P("tm", "space", None, None), P("tm", "space", None), P("tm", None)),
        check_vma=False,
    )
```

```python
import functools

import jax
import jax.numpy as jnp
from jax import lax
from jax.experimental import pallas as pl
from jax.experimental.pallas import tpu as pltpu
from jax.sharding import PartitionSpec as P

MEMS = 3
POINTERS = 16
BLOCK_ORDER = (1, 2, 0, 3)
MESH = pl.DeviceIdType.MESH
F32 = jnp.float32
BF16 = jnp.bfloat16


def mm(a, b):
    return jnp.dot(a, b, preferred_element_type=F32)


def mm_t(a, b):
    return lax.dot_general(a, b, (((1,), (1,)), ((), ())), preferred_element_type=F32)


def kernel(
    frames,
    features,
    masks_in,
    mask_embed_in,
    mem_tpos_in,
    ptr_tpos_in,
    empty_memory_in,
    w_pix,
    w_conv,
    w_out_t,
    w_ptr,
    w_query,
    w_key,
    w_value,
    w_proj,
    attended,
    memory,
    pointers,
    feat,
    masks,
    mask_embed,
    mem_tpos,
    ptr_tpos,
    empty_memory,
    pix,
    taps,
    outw,
    ptrw,
    queryw,
    key_pad,
    value_pad,
    projw,
    joined,
    halo,
    conv,
    part,
    part_near,
    parts_in,
    mem_rows,
    mem_send,
    edge_send,
    mem_in,
    load_sem,
    near_send,
    near_recv,
    mem_send_sem,
    mem_recv_sem,
    edge_send_sem,
    edge_recv_sem,
    part_send_sem,
    part_recv_sem,
):
    _, rows, columns, dim = features.shape
    tokens = rows * columns
    mem_dim = w_key.shape[0]
    half = tokens // 2
    parts = dim // mem_dim
    t = lax.axis_index("tm")
    s = lax.axis_index("space")
    other = 1 - s
    reach = min(POINTERS, frames - 1)
    mem_reach = min(MEMS, frames - 1)

    loads = []

    def load(src, dst):
        copy = pltpu.make_async_copy(src, dst, load_sem.at[len(loads)])
        copy.start()
        loads.append(copy)
        return copy

    feat_load = load(features.at[0], feat)
    mask_load = load(masks_in, masks)
    embed_load = load(mask_embed_in, mask_embed)
    pix_load = load(w_pix, pix)
    tap_loads = [load(w_conv.at[a], taps.at[a]) for a in range(3)]
    query_load = load(w_query, queryw)
    ptr_load = load(w_ptr, ptrw)
    out_loads = [load(w_out_t, outw.at[pl.ds(k * mem_dim, mem_dim)]) for k in range(2)]
    key_load = load(w_key, key_pad.at[pl.ds(mem_dim, mem_dim)])
    value_load = load(w_value, value_pad.at[pl.ds(mem_dim, mem_dim)])
    small_loads = [
        load(mem_tpos_in, mem_tpos),
        load(ptr_tpos_in, ptr_tpos),
        load(empty_memory_in, empty_memory),
    ]
    proj_load = load(w_proj, projw)

    barrier = pltpu.get_barrier_semaphore()
    for d in range(reach, 0, -1):

        @pl.when(t - d >= 0)
        def _(d=d):
            for to in range(2):
                pl.semaphore_signal(barrier, inc=1, device_id=(t - d, to), device_id_type=MESH)

    pl.semaphore_signal(barrier, inc=1, device_id=(t, other), device_id_type=MESH)

    blank = jnp.zeros((mem_dim, dim), BF16)
    for ref in (key_pad, value_pad):
        ref[0:mem_dim] = blank
        ref[2 * mem_dim : 3 * mem_dim] = blank
    joined[0] = jnp.zeros((columns, dim), BF16)
    joined[rows + 1] = jnp.zeros((columns, dim), BF16)
    for d in range(1, MEMS + 1):

        @pl.when(t - d < 0)
        def _(d=d):
            mem_in[d - 1] = jnp.zeros((2, half, 2 * mem_dim), BF16)

    for d in range(1, POINTERS + 1):

        @pl.when(t - d < 0)
        def _(d=d):
            parts_in[d - 1] = jnp.zeros((2, 1, dim), F32)

    mask_load.wait()
    mask_f = masks[0].astype(F32)
    spread = jnp.concatenate(
        [jnp.broadcast_to(mask_f[r : r + 1], (columns, columns)) for r in range(rows)], axis=0
    )
    token_col = lax.broadcasted_iota(jnp.int32, (tokens, columns), 0) % columns
    lane_col = lax.broadcasted_iota(jnp.int32, (tokens, columns), 1)
    mask_col = jnp.sum(jnp.where(token_col == lane_col, spread, 0.0), axis=1, keepdims=True)
    col_of = lax.broadcasted_iota(jnp.int32, (tokens, dim), 0) % columns

    feat_load.wait()
    flat = feat[...].reshape(tokens, dim)
    flat_f = flat.astype(F32)
    part[...] = jnp.sum(mask_col * flat_f, axis=0, keepdims=True)
    pix_load.wait()
    embed_load.wait()
    joined_rows = (
        mm(flat, pix[...]) + mask_col * mask_embed[...].astype(F32).reshape(1, dim)
    ).astype(BF16)
    joined[1 : rows + 1] = joined_rows.reshape(rows, columns, dim)

    sums = [None, None, None]
    for a in range(3):
        tap_loads[a].wait()
        window = joined[a : a + rows].reshape(tokens, dim)
        for b in range(3):
            product = mm(window, taps[a, b])
            sums[b] = product if sums[b] is None else sums[b] + product

    def shift_columns(low, mid, high, col):
        count = low.shape[0]
        low = jnp.where(col == 0, 0.0, pltpu.roll(low, 1, 0))
        high = jnp.where(col == columns - 1, 0.0, pltpu.roll(high, count - 1, 0))
        return mid + low + high

    def encode(v):
        gelu = 0.5 * v * (1.0 + jnp.tanh(0.7978845608 * (v + 0.044715 * (v * v * v))))
        return mm_t(gelu.astype(BF16), outw[...])

    conv_sum = shift_columns(*sums, col_of)
    conv[...] = conv_sum
    for out_load in out_loads:
        out_load.wait()
    twice = encode(conv_sum)
    lane = lax.broadcasted_iota(jnp.int32, (half, 2 * mem_dim), 1)
    mem_rows[...] = twice
    mem_send[...] = jnp.where(lane < mem_dim, twice[0:half], twice[half:tokens]).astype(BF16)

    centred = flat_f - jnp.mean(flat_f, axis=1, keepdims=True)
    query_in = (
        centred * lax.rsqrt(jnp.mean(centred * centred, axis=1, keepdims=True) + 1e-05)
    ).astype(BF16)
    query_load.wait()
    query = (mm(query_in, queryw[...]) * dim ** (-0.5)).astype(BF16)
    ptr_load.wait()
    peers = 1
    for d in range(1, reach + 1):
        peers = peers + (1 - (t + d) // frames) * 2
    pl.semaphore_wait(barrier, peers)

    def send(src, dst, send_sem, recv_sem, frame, to):
        return pltpu.make_async_remote_copy(
            src_ref=src,
            dst_ref=dst,
            send_sem=send_sem,
            recv_sem=recv_sem,
            device_id=(frame, to),
            device_id_type=MESH,
        )

    def part_copy(d, band, to):
        return send(
            part,
            parts_in.at[d - 1, band],
            part_send_sem.at[d - 1, to],
            part_recv_sem.at[d - 1, band],
            t + d,
            to,
        )

    main = half - columns

    def main_copy(d, band, to):
        at = pl.ds(pl.multiple_of(band * columns, columns), main)
        return send(
            mem_send.at[at],
            mem_in.at[d - 1, band, at],
            mem_send_sem.at[d - 1, to],
            mem_recv_sem.at[d - 1, band],
            t + d,
            to,
        )

    def edge_copy(d, band, to):
        at = pl.ds(pl.multiple_of((1 - band) * main, columns), columns)
        return send(
            edge_send,
            mem_in.at[d - 1, band, at],
            edge_send_sem.at[d - 1, to],
            edge_recv_sem.at[d - 1, band],
            t + d,
            to,
        )

    edge_at = pl.multiple_of(other * (tokens - columns), columns)
    edge_rows = pl.ds(edge_at, columns)
    halo_copy = send(
        joined.at[1 + other * (rows - 1)], halo, near_send.at[1], near_recv.at[1], t, other
    )
    halo_copy.start()
    for d in range(reach, 0, -1):

        @pl.when(t + d < frames)
        def _(d=d):
            for to in range(2):
                part_copy(d, s, to).start()

    for d in range(mem_reach, 0, -1):

        @pl.when(t + d < frames)
        def _(d=d):
            for to in range(2):
                main_copy(d, s, to).start()

    near_copy = send(part, part_near, near_send.at[0], near_recv.at[0], t, other)
    near_copy.start()

    key_load.wait()
    value_load.wait()
    for small_load in small_loads:
        small_load.wait()
    key_w = key_pad[mem_dim : 2 * mem_dim]
    value_w = value_pad[mem_dim : 2 * mem_dim]
    mem_tpos_keys = mm(mem_tpos[...], key_w)

    def cut(pointer_rows):
        return jnp.concatenate(
            [pointer_rows[:, j * mem_dim : (j + 1) * mem_dim] for j in range(parts)], axis=0
        )

    ptr_tokens = parts * POINTERS
    ptr_tpos_keys = mm(cut(ptr_tpos[...]), key_w)
    null_rows = jnp.broadcast_to(
        empty_memory[...].astype(F32).reshape(1, mem_dim), (ptr_tokens, mem_dim)
    ).astype(BF16)
    null_keys = mm(null_rows, key_w).astype(BF16)
    null_values = mm(null_rows, value_w).astype(BF16)

    halo_copy.wait()
    tap = 2 * other
    edge = [mm(halo[...], taps[tap, b]) for b in range(3)]
    edge_twice = encode(conv[edge_rows] + shift_columns(*edge, col_of[0:columns]))
    slab = mem_send[pl.ds(pl.multiple_of(other * main, columns), columns)].astype(F32)
    side = (lane[0:columns] // mem_dim) == other
    edge_send[...] = jnp.where(side, edge_twice, slab).astype(BF16)
    for d in range(mem_reach, 0, -1):

        @pl.when(t + d < frames)
        def _(d=d):
            for to in range(2):
                edge_copy(d, s, to).start()

    mem_rows[edge_rows] = edge_twice
    for c in range(0, columns, 2):
        even = mem_rows[pl.ds(c, rows, stride=columns), :]
        odd = mem_rows[pl.ds(c + 1, rows, stride=columns), :]
        memory[0, :, c * mem_dim : (c + 2) * mem_dim] = jnp.where(
            lane[0:rows] < mem_dim, even, odd
        ).astype(BF16)

    def to_pointers(pooled):
        normed = pooled * lax.rsqrt(jnp.mean(pooled * pooled, axis=1, keepdims=True) + 1e-06)
        return mm(normed.astype(BF16), ptrw[...]).astype(BF16)

    near_copy.wait()
    pointers[...] = to_pointers(jnp.broadcast_to(part[...] + part_near[...], (8, dim)))[0:1]

    key_low, key_high = key_pad[mem_dim : 3 * mem_dim], key_pad[0 : 2 * mem_dim]
    value_low, value_high = value_pad[mem_dim : 3 * mem_dim], value_pad[0 : 2 * mem_dim]

    def block(keys, vals, valid):
        found = jnp.where(valid, mm_t(query, keys), -1e30)
        top = jnp.max(found, axis=1, keepdims=True)
        grown = jnp.exp(found - top)
        return top, jnp.sum(grown, axis=1, keepdims=True), mm(grown.astype(BF16), vals)

    def memory_block(d):
        @pl.when(t - d >= 0)
        def _():
            for band in range(2):
                main_copy(d, band, other).wait_recv()
                edge_copy(d, band, other).wait_recv()

        packed = mem_in[d - 1].reshape(tokens, 2 * mem_dim)
        tpos = mem_tpos_keys[d - 1 : d]
        keys = [(mm(packed, w) + tpos).astype(BF16) for w in (key_low, key_high)]
        vals = [mm(packed, w).astype(BF16) for w in (value_low, value_high)]
        return block(jnp.concatenate(keys, axis=0), jnp.concatenate(vals, axis=0), t - d >= 0)

    def pointer_block():
        for d in range(1, reach + 1):

            @pl.when(t - d >= 0)
            def _(d=d):
                for band in range(2):
                    part_copy(d, band, other).wait_recv()

        tokens_in = cut(to_pointers((parts_in[:, 0] + parts_in[:, 1]).reshape(POINTERS, dim)))
        keys = jnp.concatenate(
            [(mm(tokens_in, key_w) + ptr_tpos_keys).astype(BF16), null_keys], axis=0
        )
        vals = jnp.concatenate([mm(tokens_in, value_w).astype(BF16), null_values], axis=0)
        index = lax.broadcasted_iota(jnp.int32, (1, 2 * ptr_tokens), 1)
        oldest = t - 1 - index % POINTERS
        valid = ((index < ptr_tokens) & (oldest >= 0)) | (index == ptr_tokens)
        return block(keys, vals, valid)

    blocks = [pointer_block() if d == 0 else memory_block(d) for d in BLOCK_ORDER]
    top = functools.reduce(jnp.maximum, [b[0] for b in blocks])
    factors = [jnp.exp(b[0] - top) for b in blocks]
    total = sum(f * b[1] for f, b in zip(factors, blocks))
    scale = 1.0 / total
    mixed = sum((f * scale) * b[2] for f, b in zip(factors, blocks)).astype(BF16)
    proj_load.wait()
    result = feat[...].reshape(tokens, dim).astype(F32) + mm(mixed, projw[...])
    attended[0] = result.astype(BF16).reshape(rows, columns, dim)

    for d in range(1, reach + 1):

        @pl.when(t + d < frames)
        def _(d=d):
            for to in range(2):
                part_copy(d, s, to).wait_send()
                if d <= mem_reach:
                    main_copy(d, s, to).wait_send()
                    edge_copy(d, s, to).wait_send()


def from_behind(block, axis, distance):
    devices = range(lax.axis_size(axis))
    route = [(i - distance, i) for i in devices if i - distance in devices]
    return lax.ppermute(block, axis, route)


def with_halo(block, sides, width):
    for axis, dim in sides:
        count = lax.axis_size(axis)
        forward = [(i, i + 1) for i in range(count - 1)]
        backward = [(target, source) for source, target in forward]
        low = lax.ppermute(
            lax.slice_in_dim(block, block.shape[dim] - width, None, axis=dim), axis, forward
        )
        high = lax.ppermute(lax.slice_in_dim(block, 0, width, axis=dim), axis, backward)
        block = jnp.concatenate([low, block, high], axis=dim)
    return block


def fetch_earlier(carried, hop_count):
    pieces = []
    for step_index in range(hop_count):
        pieces.append(from_behind(carried, "tm", step_index + 1))
    return jnp.concatenate(pieces[::-1], axis=0)


def attend(query, blocks):
    scores = []
    row_top = None
    for key_rows, value_rows, is_valid in blocks:
        block_scores = lax.dot_general(
            query, key_rows, (((1,), (1,)), ((), ())), preferred_element_type=jnp.float32
        )
        block_scores = jnp.where(is_valid, block_scores, -jnp.inf)
        scores.append(block_scores)
        block_top = jnp.max(block_scores, axis=1, keepdims=True)
        row_top = block_top if row_top is None else jnp.maximum(row_top, block_top)
    row_total = jnp.zeros_like(row_top)
    for block_scores in scores:
        row_total = row_total + jnp.sum(jnp.exp(block_scores - row_top), axis=1, keepdims=True)
    mixed_sum = jnp.zeros((query.shape[0], blocks[0][1].shape[1]), jnp.float32)
    for block_scores, block in zip(scores, blocks):
        weights = (jnp.exp(block_scores - row_top) / row_total).astype(jnp.bfloat16)
        mixed_sum = mixed_sum + jnp.dot(weights, block[1], preferred_element_type=jnp.float32)
    return mixed_sum.astype(jnp.bfloat16)


def staged_body(
    features,
    masks,
    w_pix,
    mask_embed,
    w_conv,
    w_out,
    w_ptr,
    w_query,
    w_key,
    w_value,
    w_proj,
    mem_tpos,
    ptr_tpos,
    empty_memory,
):
    frames_dev, rows_dev, columns, model_dim = features.shape
    mem_dim = w_key.shape[0]
    ptr_tok = model_dim // mem_dim
    band_tokens = rows_dev * columns
    flat_rows = features.reshape(frames_dev * band_tokens, model_dim)
    mask_rows = masks.reshape(frames_dev * band_tokens, 1).astype(jnp.float32)
    joined_map = (
        jnp.dot(flat_rows, w_pix, preferred_element_type=jnp.float32)
        + mask_rows * mask_embed.astype(jnp.float32)
    ).astype(jnp.bfloat16)
    joined_map = joined_map.reshape(frames_dev, rows_dev, columns, model_dim)
    padded = with_halo(joined_map, (("space", 1),), 1)
    padded = jnp.pad(padded, ((0, 0), (0, 0), (1, 1), (0, 0)))
    conv_sum = jnp.zeros((frames_dev * band_tokens, model_dim), jnp.float32)
    for row_tap in range(3):
        for col_tap in range(3):
            window_rows = padded[
                :, row_tap : row_tap + rows_dev, col_tap : col_tap + columns, :
            ].reshape(-1, model_dim)
            conv_sum = conv_sum + jnp.dot(
                window_rows, w_conv[row_tap, col_tap], preferred_element_type=jnp.float32
            )
    hidden = jax.nn.gelu(conv_sum, approximate=True).astype(jnp.bfloat16)
    memory = jnp.dot(hidden, w_out, preferred_element_type=jnp.float32).astype(jnp.bfloat16)
    memory = memory.reshape(frames_dev, rows_dev, columns * mem_dim)
    band_mask = masks.reshape(frames_dev, band_tokens).astype(jnp.bfloat16)
    partial_value = jnp.einsum(
        "ft,ftd->fd",
        band_mask,
        features.reshape(frames_dev, band_tokens, model_dim),
        preferred_element_type=jnp.float32,
    )
    pooled = lax.psum(partial_value, "space")
    normed = (pooled * lax.rsqrt(jnp.mean(pooled * pooled, axis=1, keepdims=True) + 1e-06)).astype(
        jnp.bfloat16
    )
    pointers = jnp.dot(normed, w_ptr, preferred_element_type=jnp.float32).astype(jnp.bfloat16)
    all_pointers = lax.all_gather(pointers, "tm", axis=0, tiled=True)
    hop_count = (MEMS + frames_dev - 1) // frames_dev
    carried = lax.all_gather(memory, "space", axis=1, tiled=True)
    history = jnp.concatenate(
        [fetch_earlier(carried, hop_count), carried[: frames_dev - 1]], axis=0
    )
    grid_tokens = columns * columns
    hist_frames = history.shape[0]
    history = history.reshape(hist_frames, grid_tokens, mem_dim)
    hist_values = jnp.dot(
        history.reshape(-1, mem_dim), w_value, preferred_element_type=jnp.float32
    ).astype(jnp.bfloat16)
    hist_values = hist_values.reshape(hist_frames, grid_tokens, model_dim)
    tpos_keys = jnp.dot(mem_tpos, w_key, preferred_element_type=jnp.float32)
    ptr_tpos_keys = jnp.dot(
        ptr_tpos[::-1].reshape(POINTERS * ptr_tok, mem_dim),
        w_key,
        preferred_element_type=jnp.float32,
    )
    null_key = jnp.dot(
        empty_memory.reshape(1, mem_dim), w_key, preferred_element_type=jnp.float32
    ).astype(jnp.bfloat16)
    null_value = jnp.dot(
        empty_memory.reshape(1, mem_dim), w_value, preferred_element_type=jnp.float32
    ).astype(jnp.bfloat16)
    padded_ptr = jnp.concatenate(
        [jnp.zeros((POINTERS, model_dim), jnp.bfloat16), all_pointers], axis=0
    )
    ptr_offsets = jnp.repeat(jnp.arange(POINTERS, dtype=jnp.int32) - POINTERS, ptr_tok)
    features_f = features.reshape(frames_dev, band_tokens, model_dim).astype(jnp.float32)
    first_frame = lax.axis_index("tm") * frames_dev
    frame = first_frame + 0
    rows_f = features_f[0]
    centred = rows_f - jnp.mean(rows_f, axis=1, keepdims=True)
    query_in = (
        centred * lax.rsqrt(jnp.mean(centred * centred, axis=1, keepdims=True) + 1e-05)
    ).astype(jnp.bfloat16)
    query = (
        jnp.dot(query_in, w_query, preferred_element_type=jnp.float32) * model_dim ** (-0.5)
    ).astype(jnp.bfloat16)
    blocks = []
    for distance in range(1, MEMS + 1):
        slot_index = hop_count * frames_dev - distance
        key_rows = (
            jnp.dot(history[slot_index], w_key, preferred_element_type=jnp.float32)
            + tpos_keys[distance - 1]
        ).astype(jnp.bfloat16)
        blocks.append((key_rows, hist_values[slot_index], frame - distance >= 0))
    window = lax.dynamic_slice_in_dim(padded_ptr, frame, POINTERS, 0)
    ptr_tokens = window.reshape(POINTERS * ptr_tok, mem_dim)
    ptr_keys = (
        jnp.dot(ptr_tokens, w_key, preferred_element_type=jnp.float32) + ptr_tpos_keys
    ).astype(jnp.bfloat16)
    ptr_values = jnp.dot(ptr_tokens, w_value, preferred_element_type=jnp.float32).astype(
        jnp.bfloat16
    )
    extra_valid = jnp.concatenate([frame + ptr_offsets >= 0, jnp.ones((1,), bool)], axis=0)
    blocks.append(
        (
            jnp.concatenate([ptr_keys, null_key], axis=0),
            jnp.concatenate([ptr_values, null_value], axis=0),
            extra_valid[None, :],
        )
    )
    mixed_rows = attend(query, blocks)
    outputs = [
        (rows_f + jnp.dot(mixed_rows, w_proj, preferred_element_type=jnp.float32)).astype(
            jnp.bfloat16
        )
    ]
    attended = jnp.stack(outputs, axis=0).reshape(frames_dev, rows_dev, columns, model_dim)
    return (attended, memory, pointers)


def put_out(*refs):
    sem = refs[-1]
    copies = [pltpu.make_async_copy(refs[k], refs[3 + k], sem.at[k]) for k in range(3)]
    for copy in copies:
        copy.start()
    for copy in copies:
        copy.wait()


def fused_body(
    features,
    masks,
    w_pix,
    mask_embed,
    w_conv,
    w_out,
    w_ptr,
    w_query,
    w_key,
    w_value,
    w_proj,
    mem_tpos,
    ptr_tpos,
    empty_memory,
):
    _, rows, columns, dim = features.shape
    frames = lax.axis_size("tm")
    mem_dim = w_key.shape[0]
    tokens = rows * columns
    half = tokens // 2
    vmem = pl.BlockSpec(memory_space=pltpu.VMEM)
    hbm = pl.BlockSpec(memory_space=pltpu.HBM)
    dma = pltpu.SemaphoreType.DMA
    results = pl.pallas_call(
        functools.partial(kernel, frames),
        out_shape=(
            pltpu.VMEM(features.shape, BF16),
            pltpu.VMEM((1, rows, columns * mem_dim), BF16),
            pltpu.VMEM((1, dim), BF16),
        ),
        in_specs=[hbm] * 14,
        out_specs=(vmem, vmem, vmem),
        scratch_shapes=[
            pltpu.VMEM((rows, columns, dim), BF16),
            pltpu.VMEM(masks.shape, masks.dtype),
            pltpu.VMEM(mask_embed.shape, BF16),
            pltpu.VMEM(mem_tpos.shape, BF16),
            pltpu.VMEM(ptr_tpos.shape, BF16),
            pltpu.VMEM(empty_memory.shape, BF16),
            pltpu.VMEM(w_pix.shape, BF16),
            pltpu.VMEM(w_conv.shape, BF16),
            pltpu.VMEM((2 * mem_dim, dim), BF16),
            pltpu.VMEM(w_ptr.shape, BF16),
            pltpu.VMEM(w_query.shape, BF16),
            pltpu.VMEM((3 * mem_dim, dim), BF16),
            pltpu.VMEM((3 * mem_dim, dim), BF16),
            pltpu.VMEM(w_proj.shape, BF16),
            pltpu.VMEM((rows + 2, columns, dim), BF16),
            pltpu.VMEM((columns, dim), BF16),
            pltpu.VMEM((tokens, dim), F32),
            pltpu.VMEM((1, dim), F32),
            pltpu.VMEM((1, dim), F32),
            pltpu.VMEM((POINTERS, 2, 1, dim), F32),
            pltpu.VMEM((tokens, 2 * mem_dim), F32),
            pltpu.VMEM((half, 2 * mem_dim), BF16),
            pltpu.VMEM((columns, 2 * mem_dim), BF16),
            pltpu.VMEM((MEMS, 2, half, 2 * mem_dim), BF16),
            dma((17,)),
            dma((2,)),
            dma((2,)),
            dma((MEMS, 2)),
            dma((MEMS, 2)),
            dma((MEMS, 2)),
            dma((MEMS, 2)),
            dma((POINTERS, 2)),
            dma((POINTERS, 2)),
        ],
        compiler_params=pltpu.CompilerParams(
            collective_id=0, has_side_effects=True
        ),
    )(
        features,
        masks,
        mask_embed,
        mem_tpos,
        ptr_tpos,
        empty_memory,
        w_pix,
        w_conv,
        w_out.T,
        w_ptr,
        w_query,
        w_key,
        w_value,
        w_proj,
    )
    return pl.pallas_call(
        put_out,
        out_shape=tuple(jax.ShapeDtypeStruct(x.shape, x.dtype) for x in results),
        in_specs=[vmem] * 3,
        out_specs=(hbm,) * 3,
        scratch_shapes=[dma((3,))],
        compiler_params=pltpu.CompilerParams(vmem_limit_bytes=2**20),
    )(*[pltpu.with_memory_space_constraint(x, pltpu.VMEM) for x in results])


def body(features, *rest):
    frames_dev, rows, columns, dim = features.shape
    key_count = MEMS * 2 * rows * columns
    fits = rows * columns * key_count * 4 <= 2**23 and rows * columns <= 256
    if frames_dev == 1 and lax.axis_size("space") == 2 and fits:
        return fused_body(features, *rest)
    return staged_body(features, *rest)


def solution(mesh):
    return jax.shard_map(
        body,
        mesh=mesh,
        in_specs=(P("tm", "space", None, None), P("tm", "space", None)) + (P(),) * 12,
        out_specs=(P("tm", "space", None, None), P("tm", "space", None), P("tm", None)),
        check_vma=False,
    )
```

```python
import functools

import jax
import jax.numpy as jnp
from jax import lax
from jax.experimental import pallas as pl
from jax.experimental.pallas import tpu as pltpu
from jax.sharding import PartitionSpec as P

MEMS = 3
POINTERS = 16
BLOCK_ORDER = (1, 2, 0, 3)
MESH = pl.DeviceIdType.MESH
F32 = jnp.float32
BF16 = jnp.bfloat16


def stride_of(frames):
    return max(k for k in range(1, frames + 1) if frames % k == 0 and k * k <= frames)


def mm(a, b):
    return jnp.dot(a, b, preferred_element_type=F32)


def mm_t(a, b):
    return lax.dot_general(a, b, (((1,), (1,)), ((), ())), preferred_element_type=F32)


def kernel(
    frames,
    features,
    masks_in,
    mask_embed_in,
    mem_tpos_in,
    ptr_tpos_in,
    empty_memory_in,
    w_pix,
    w_conv,
    w_out_t,
    w_ptr,
    w_query,
    w_key,
    w_value,
    w_proj,
    attended,
    memory,
    pointers,
    feat,
    masks,
    mask_embed,
    mem_tpos,
    ptr_tpos,
    empty_memory,
    pix,
    taps,
    outw,
    ptrw,
    queryw,
    key_pad,
    value_pad,
    projw,
    joined,
    halo,
    conv,
    part,
    table,
    mem_rows,
    mem_send,
    edge_send,
    mem_in,
    load_sem,
    near_send,
    near_recv,
    mem_send_sem,
    mem_recv_sem,
    edge_send_sem,
    edge_recv_sem,
    part_send_sem,
    part_recv_sem,
    row_send_sem,
    row_recv_sem,
):
    _, rows, columns, dim = features.shape
    tokens = rows * columns
    mem_dim = w_key.shape[0]
    half = tokens // 2
    parts = dim // mem_dim
    t = lax.axis_index("tm")
    s = lax.axis_index("space")
    other = 1 - s
    group = stride_of(frames)
    stripes = frames // group
    place, stripe = t % group, t // group
    fan = {}
    for offset in range(1 - frames, frames):
        if 1 <= offset <= MEMS or 0 < abs(offset) < group:
            fan[offset] = 2
        elif offset > 0 and offset % group == 0:
            fan[offset] = 1
    mem_reach = min(MEMS, frames - 1)

    loads = []

    def load(src, dst):
        copy = pltpu.make_async_copy(src, dst, load_sem.at[len(loads)])
        copy.start()
        loads.append(copy)
        return copy

    feat_load = load(features.at[0], feat)
    mask_load = load(masks_in, masks)
    embed_load = load(mask_embed_in, mask_embed)
    pix_load = load(w_pix, pix)
    tap_loads = [load(w_conv.at[a], taps.at[a]) for a in range(3)]
    query_load = load(w_query, queryw)
    ptr_load = load(w_ptr, ptrw)
    out_loads = [load(w_out_t, outw.at[pl.ds(k * mem_dim, mem_dim)]) for k in range(2)]
    key_load = load(w_key, key_pad.at[pl.ds(mem_dim, mem_dim)])
    value_load = load(w_value, value_pad.at[pl.ds(mem_dim, mem_dim)])
    small_loads = [
        load(mem_tpos_in, mem_tpos),
        load(ptr_tpos_in, ptr_tpos),
        load(empty_memory_in, empty_memory),
    ]
    proj_load = load(w_proj, projw)

    barrier = pltpu.get_barrier_semaphore()
    for offset in sorted(fan, reverse=True):
        inside = (place - offset >= 0) & (place - offset < group)

        @pl.when(t - offset >= 0 if offset > 0 and (offset <= MEMS or offset >= group) else inside)
        def _(offset=offset):
            for to in range(2) if fan[offset] == 2 else (s,):
                pl.semaphore_signal(
                    barrier, inc=1, device_id=(t - offset, to), device_id_type=MESH
                )

    pl.semaphore_signal(barrier, inc=1, device_id=(t, other), device_id_type=MESH)

    blank = jnp.zeros((mem_dim, dim), BF16)
    for ref in (key_pad, value_pad):
        ref[0:mem_dim] = blank
        ref[2 * mem_dim : 3 * mem_dim] = blank
    joined[0] = jnp.zeros((columns, dim), BF16)
    joined[rows + 1] = jnp.zeros((columns, dim), BF16)
    for d in range(1, MEMS + 1):

        @pl.when(t - d < 0)
        def _(d=d):
            mem_in[d - 1] = jnp.zeros((2, half, 2 * mem_dim), BF16)

    for k in range(1, stripes):

        @pl.when(k > stripe)
        def _(k=k):
            table[s, place, k] = jnp.zeros((1, dim), F32)

    mask_load.wait()
    mask_f = masks[0].astype(F32)
    spread = jnp.concatenate(
        [jnp.broadcast_to(mask_f[r : r + 1], (columns, columns)) for r in range(rows)], axis=0
    )
    token_col = lax.broadcasted_iota(jnp.int32, (tokens, columns), 0) % columns
    lane_col = lax.broadcasted_iota(jnp.int32, (tokens, columns), 1)
    mask_col = jnp.sum(jnp.where(token_col == lane_col, spread, 0.0), axis=1, keepdims=True)
    col_of = lax.broadcasted_iota(jnp.int32, (tokens, dim), 0) % columns

    feat_load.wait()
    flat = feat[...].reshape(tokens, dim)
    flat_f = flat.astype(F32)
    pooled_part = jnp.sum(mask_col * flat_f, axis=0, keepdims=True)
    part[...] = pooled_part
    table[s, place, stripe] = pooled_part
    pix_load.wait()
    embed_load.wait()
    joined_rows = (
        mm(flat, pix[...]) + mask_col * mask_embed[...].astype(F32).reshape(1, dim)
    ).astype(BF16)
    joined[1 : rows + 1] = joined_rows.reshape(rows, columns, dim)

    sums = [None, None, None]
    for a in range(3):
        tap_loads[a].wait()
        window = joined[a : a + rows].reshape(tokens, dim)
        for b in range(3):
            product = mm(window, taps[a, b])
            sums[b] = product if sums[b] is None else sums[b] + product

    def shift_columns(low, mid, high, col):
        count = low.shape[0]
        low = jnp.where(col == 0, 0.0, pltpu.roll(low, 1, 0))
        high = jnp.where(col == columns - 1, 0.0, pltpu.roll(high, count - 1, 0))
        return mid + low + high

    def encode(v):
        gelu = 0.5 * v * (1.0 + jnp.tanh(0.7978845608 * (v + 0.044715 * (v * v * v))))
        return mm_t(gelu.astype(BF16), outw[...])

    conv_sum = shift_columns(*sums, col_of)
    conv[...] = conv_sum
    for out_load in out_loads:
        out_load.wait()
    twice = encode(conv_sum)
    lane = lax.broadcasted_iota(jnp.int32, (half, 2 * mem_dim), 1)
    mem_rows[...] = twice
    mem_send[...] = jnp.where(lane < mem_dim, twice[0:half], twice[half:tokens]).astype(BF16)

    centred = flat_f - jnp.mean(flat_f, axis=1, keepdims=True)
    query_in = (
        centred * lax.rsqrt(jnp.mean(centred * centred, axis=1, keepdims=True) + 1e-05)
    ).astype(BF16)
    query_load.wait()
    query = (mm(query_in, queryw[...]) * dim ** (-0.5)).astype(BF16)
    ptr_load.wait()
    peers = 1
    for offset, cores in fan.items():
        if offset > 0 and (offset <= MEMS or offset >= group):
            peers = peers + (1 - (t + offset) // frames) * cores
        elif offset > 0:
            peers = peers + (1 - (place + offset) // group) * cores
        else:
            peers = peers + ((place + offset + group) // group) * cores
    pl.semaphore_wait(barrier, peers)

    def send(src, dst, send_sem, recv_sem, frame, to):
        return pltpu.make_async_remote_copy(
            src_ref=src,
            dst_ref=dst,
            send_sem=send_sem,
            recv_sem=recv_sem,
            device_id=(frame, to),
            device_id_type=MESH,
        )

    def stripe_copy(hop, k):
        return send(
            part,
            table.at[s, place, k],
            part_send_sem.at[hop],
            part_recv_sem.at[k],
            t + hop * group,
            s,
        )

    def row_copy(shift, band, to):
        at = table.at[band, (place - shift + group) % group if to is None else place]
        return send(
            at,
            at,
            row_send_sem.at[shift, band if to is None else to],
            row_recv_sem.at[shift, band],
            stripe * group + (place + shift) % group,
            other if to is None else to,
        )

    main = half - columns

    def main_copy(d, band, to):
        at = pl.ds(pl.multiple_of(band * columns, columns), main)
        return send(
            mem_send.at[at],
            mem_in.at[d - 1, band, at],
            mem_send_sem.at[d - 1, to],
            mem_recv_sem.at[d - 1, band],
            t + d,
            to,
        )

    def edge_copy(d, band, to):
        at = pl.ds(pl.multiple_of((1 - band) * main, columns), columns)
        return send(
            edge_send,
            mem_in.at[d - 1, band, at],
            edge_send_sem.at[d - 1, to],
            edge_recv_sem.at[d - 1, band],
            t + d,
            to,
        )

    edge_at = pl.multiple_of(other * (tokens - columns), columns)
    edge_rows = pl.ds(edge_at, columns)
    halo_copy = send(
        joined.at[1 + other * (rows - 1)], halo, near_send, near_recv, t, other
    )
    halo_copy.start()
    for hop in range(stripes - 1, 0, -1):

        @pl.when(t + hop * group < frames)
        def _(hop=hop):
            stripe_copy(hop, stripe).start()

    for d in range(mem_reach, 0, -1):

        @pl.when(t + d < frames)
        def _(d=d):
            for to in range(2):
                main_copy(d, s, to).start()

    key_load.wait()
    value_load.wait()
    for small_load in small_loads:
        small_load.wait()
    key_w = key_pad[mem_dim : 2 * mem_dim]
    value_w = value_pad[mem_dim : 2 * mem_dim]
    mem_tpos_keys = mm(mem_tpos[...], key_w)

    def cut(pointer_rows):
        return jnp.concatenate(
            [pointer_rows[:, j * mem_dim : (j + 1) * mem_dim] for j in range(parts)], axis=0
        )

    ptr_tokens = parts * frames
    row_id = lax.broadcasted_iota(jnp.int32, (frames, POINTERS), 0)
    row_age = t - 1 - ((row_id % stripes) * group + row_id // stripes)
    pick = row_age == lax.broadcasted_iota(jnp.int32, (frames, POINTERS), 1)
    aged_tpos = mm(jnp.where(pick, 1.0, 0.0).astype(BF16), ptr_tpos[...]).astype(BF16)
    ptr_tpos_keys = mm(cut(aged_tpos), key_w)
    null_rows = jnp.broadcast_to(
        empty_memory[...].astype(F32).reshape(1, mem_dim), (ptr_tokens, mem_dim)
    ).astype(BF16)
    null_keys = mm(null_rows, key_w).astype(BF16)
    null_values = mm(null_rows, value_w).astype(BF16)

    def relay():
        for k in range(stripes - 1):

            @pl.when(k < stripe)
            def _(k=k):
                stripe_copy(1, k).wait_recv()

        for shift in range(group - 1, -1, -1):
            for to in range(2) if shift else (other,):
                row_copy(shift, s, to).start()

    halo_copy.wait()
    tap = 2 * other
    edge = [mm(halo[...], taps[tap, b]) for b in range(3)]
    edge_twice = encode(conv[edge_rows] + shift_columns(*edge, col_of[0:columns]))
    slab = mem_send[pl.ds(pl.multiple_of(other * main, columns), columns)].astype(F32)
    side = (lane[0:columns] // mem_dim) == other
    edge_send[...] = jnp.where(side, edge_twice, slab).astype(BF16)
    for d in range(mem_reach, 0, -1):

        @pl.when(t + d < frames)
        def _(d=d):
            for to in range(2):
                edge_copy(d, s, to).start()

    mem_rows[edge_rows] = edge_twice
    relay()
    for c in range(0, columns, 2):
        even = mem_rows[pl.ds(c, rows, stride=columns), :]
        odd = mem_rows[pl.ds(c + 1, rows, stride=columns), :]
        memory[0, :, c * mem_dim : (c + 2) * mem_dim] = jnp.where(
            lane[0:rows] < mem_dim, even, odd
        ).astype(BF16)

    def to_pointers(pooled):
        normed = pooled * lax.rsqrt(jnp.mean(pooled * pooled, axis=1, keepdims=True) + 1e-06)
        return mm(normed.astype(BF16), ptrw[...]).astype(BF16)

    key_low, key_high = key_pad[mem_dim : 3 * mem_dim], key_pad[0 : 2 * mem_dim]
    value_low, value_high = value_pad[mem_dim : 3 * mem_dim], value_pad[0 : 2 * mem_dim]

    def block(keys, vals, valid):
        found = jnp.where(valid, mm_t(query, keys), -1e30)
        top = jnp.max(found, axis=1, keepdims=True)
        grown = jnp.exp(found - top)
        return top, jnp.sum(grown, axis=1, keepdims=True), mm(grown.astype(BF16), vals)

    def memory_block(d):
        @pl.when(t - d >= 0)
        def _():
            for band in range(2):
                main_copy(d, band, other).wait_recv()
                edge_copy(d, band, other).wait_recv()

        packed = mem_in[d - 1].reshape(tokens, 2 * mem_dim)
        tpos = mem_tpos_keys[d - 1 : d]
        keys = [(mm(packed, w) + tpos).astype(BF16) for w in (key_low, key_high)]
        vals = [mm(packed, w).astype(BF16) for w in (value_low, value_high)]
        return block(jnp.concatenate(keys, axis=0), jnp.concatenate(vals, axis=0), t - d >= 0)

    def pointer_block():
        for shift in range(group):
            for band in range(2) if shift else (other,):
                row_copy(shift, band, None).wait_recv()

        own = table[0, place, stripe] + table[1, place, stripe]
        pointers[...] = to_pointers(jnp.broadcast_to(own, (8, dim)))[0:1]
        pooled = (table[0] + table[1]).reshape(frames, dim)
        tokens_in = cut(to_pointers(pooled))
        keys = jnp.concatenate(
            [(mm(tokens_in, key_w) + ptr_tpos_keys).astype(BF16), null_keys], axis=0
        )
        vals = jnp.concatenate([mm(tokens_in, value_w).astype(BF16), null_values], axis=0)
        index = lax.broadcasted_iota(jnp.int32, (1, 2 * ptr_tokens), 1)
        row = index % frames
        age = t - 1 - ((row % stripes) * group + row // stripes)
        known = (age >= 0) & (age < POINTERS)
        valid = ((index < ptr_tokens) & known) | (index == ptr_tokens)
        return block(keys, vals, valid)

    blocks = [pointer_block() if d == 0 else memory_block(d) for d in BLOCK_ORDER]
    top = functools.reduce(jnp.maximum, [b[0] for b in blocks])
    factors = [jnp.exp(b[0] - top) for b in blocks]
    total = sum(f * b[1] for f, b in zip(factors, blocks))
    scale = 1.0 / total
    mixed = sum((f * scale) * b[2] for f, b in zip(factors, blocks)).astype(BF16)
    proj_load.wait()
    result = feat[...].reshape(tokens, dim).astype(F32) + mm(mixed, projw[...])
    attended[0] = result.astype(BF16).reshape(rows, columns, dim)

    for hop in range(1, stripes):

        @pl.when(t + hop * group < frames)
        def _(hop=hop):
            stripe_copy(hop, stripe).wait_send()

    for shift in range(group):
        for to in range(2) if shift else (other,):
            row_copy(shift, s, to).wait_send()

    for d in range(1, mem_reach + 1):

        @pl.when(t + d < frames)
        def _(d=d):
            for to in range(2):
                main_copy(d, s, to).wait_send()
                edge_copy(d, s, to).wait_send()


def from_behind(block, axis, distance):
    devices = range(lax.axis_size(axis))
    route = [(i - distance, i) for i in devices if i - distance in devices]
    return lax.ppermute(block, axis, route)


def with_halo(block, sides, width):
    for axis, dim in sides:
        count = lax.axis_size(axis)
        forward = [(i, i + 1) for i in range(count - 1)]
        backward = [(target, source) for source, target in forward]
        low = lax.ppermute(
            lax.slice_in_dim(block, block.shape[dim] - width, None, axis=dim), axis, forward
        )
        high = lax.ppermute(lax.slice_in_dim(block, 0, width, axis=dim), axis, backward)
        block = jnp.concatenate([low, block, high], axis=dim)
    return block


def fetch_earlier(carried, hop_count):
    pieces = []
    for step_index in range(hop_count):
        pieces.append(from_behind(carried, "tm", step_index + 1))
    return jnp.concatenate(pieces[::-1], axis=0)


def attend(query, blocks):
    scores = []
    row_top = None
    for key_rows, value_rows, is_valid in blocks:
        block_scores = lax.dot_general(
            query, key_rows, (((1,), (1,)), ((), ())), preferred_element_type=jnp.float32
        )
        block_scores = jnp.where(is_valid, block_scores, -jnp.inf)
        scores.append(block_scores)
        block_top = jnp.max(block_scores, axis=1, keepdims=True)
        row_top = block_top if row_top is None else jnp.maximum(row_top, block_top)
    row_total = jnp.zeros_like(row_top)
    for block_scores in scores:
        row_total = row_total + jnp.sum(jnp.exp(block_scores - row_top), axis=1, keepdims=True)
    mixed_sum = jnp.zeros((query.shape[0], blocks[0][1].shape[1]), jnp.float32)
    for block_scores, block in zip(scores, blocks):
        weights = (jnp.exp(block_scores - row_top) / row_total).astype(jnp.bfloat16)
        mixed_sum = mixed_sum + jnp.dot(weights, block[1], preferred_element_type=jnp.float32)
    return mixed_sum.astype(jnp.bfloat16)


def staged_body(
    features,
    masks,
    w_pix,
    mask_embed,
    w_conv,
    w_out,
    w_ptr,
    w_query,
    w_key,
    w_value,
    w_proj,
    mem_tpos,
    ptr_tpos,
    empty_memory,
):
    frames_dev, rows_dev, columns, model_dim = features.shape
    mem_dim = w_key.shape[0]
    ptr_tok = model_dim // mem_dim
    band_tokens = rows_dev * columns
    flat_rows = features.reshape(frames_dev * band_tokens, model_dim)
    mask_rows = masks.reshape(frames_dev * band_tokens, 1).astype(jnp.float32)
    joined_map = (
        jnp.dot(flat_rows, w_pix, preferred_element_type=jnp.float32)
        + mask_rows * mask_embed.astype(jnp.float32)
    ).astype(jnp.bfloat16)
    joined_map = joined_map.reshape(frames_dev, rows_dev, columns, model_dim)
    padded = with_halo(joined_map, (("space", 1),), 1)
    padded = jnp.pad(padded, ((0, 0), (0, 0), (1, 1), (0, 0)))
    conv_sum = jnp.zeros((frames_dev * band_tokens, model_dim), jnp.float32)
    for row_tap in range(3):
        for col_tap in range(3):
            window_rows = padded[
                :, row_tap : row_tap + rows_dev, col_tap : col_tap + columns, :
            ].reshape(-1, model_dim)
            conv_sum = conv_sum + jnp.dot(
                window_rows, w_conv[row_tap, col_tap], preferred_element_type=jnp.float32
            )
    hidden = jax.nn.gelu(conv_sum, approximate=True).astype(jnp.bfloat16)
    memory = jnp.dot(hidden, w_out, preferred_element_type=jnp.float32).astype(jnp.bfloat16)
    memory = memory.reshape(frames_dev, rows_dev, columns * mem_dim)
    band_mask = masks.reshape(frames_dev, band_tokens).astype(jnp.bfloat16)
    partial_value = jnp.einsum(
        "ft,ftd->fd",
        band_mask,
        features.reshape(frames_dev, band_tokens, model_dim),
        preferred_element_type=jnp.float32,
    )
    pooled = lax.psum(partial_value, "space")
    normed = (pooled * lax.rsqrt(jnp.mean(pooled * pooled, axis=1, keepdims=True) + 1e-06)).astype(
        jnp.bfloat16
    )
    pointers = jnp.dot(normed, w_ptr, preferred_element_type=jnp.float32).astype(jnp.bfloat16)
    all_pointers = lax.all_gather(pointers, "tm", axis=0, tiled=True)
    hop_count = (MEMS + frames_dev - 1) // frames_dev
    carried = lax.all_gather(memory, "space", axis=1, tiled=True)
    history = jnp.concatenate(
        [fetch_earlier(carried, hop_count), carried[: frames_dev - 1]], axis=0
    )
    grid_tokens = columns * columns
    hist_frames = history.shape[0]
    history = history.reshape(hist_frames, grid_tokens, mem_dim)
    hist_values = jnp.dot(
        history.reshape(-1, mem_dim), w_value, preferred_element_type=jnp.float32
    ).astype(jnp.bfloat16)
    hist_values = hist_values.reshape(hist_frames, grid_tokens, model_dim)
    tpos_keys = jnp.dot(mem_tpos, w_key, preferred_element_type=jnp.float32)
    ptr_tpos_keys = jnp.dot(
        ptr_tpos[::-1].reshape(POINTERS * ptr_tok, mem_dim),
        w_key,
        preferred_element_type=jnp.float32,
    )
    null_key = jnp.dot(
        empty_memory.reshape(1, mem_dim), w_key, preferred_element_type=jnp.float32
    ).astype(jnp.bfloat16)
    null_value = jnp.dot(
        empty_memory.reshape(1, mem_dim), w_value, preferred_element_type=jnp.float32
    ).astype(jnp.bfloat16)
    padded_ptr = jnp.concatenate(
        [jnp.zeros((POINTERS, model_dim), jnp.bfloat16), all_pointers], axis=0
    )
    ptr_offsets = jnp.repeat(jnp.arange(POINTERS, dtype=jnp.int32) - POINTERS, ptr_tok)
    features_f = features.reshape(frames_dev, band_tokens, model_dim).astype(jnp.float32)
    first_frame = lax.axis_index("tm") * frames_dev
    frame = first_frame + 0
    rows_f = features_f[0]
    centred = rows_f - jnp.mean(rows_f, axis=1, keepdims=True)
    query_in = (
        centred * lax.rsqrt(jnp.mean(centred * centred, axis=1, keepdims=True) + 1e-05)
    ).astype(jnp.bfloat16)
    query = (
        jnp.dot(query_in, w_query, preferred_element_type=jnp.float32) * model_dim ** (-0.5)
    ).astype(jnp.bfloat16)
    blocks = []
    for distance in range(1, MEMS + 1):
        slot_index = hop_count * frames_dev - distance
        key_rows = (
            jnp.dot(history[slot_index], w_key, preferred_element_type=jnp.float32)
            + tpos_keys[distance - 1]
        ).astype(jnp.bfloat16)
        blocks.append((key_rows, hist_values[slot_index], frame - distance >= 0))
    window = lax.dynamic_slice_in_dim(padded_ptr, frame, POINTERS, 0)
    ptr_tokens = window.reshape(POINTERS * ptr_tok, mem_dim)
    ptr_keys = (
        jnp.dot(ptr_tokens, w_key, preferred_element_type=jnp.float32) + ptr_tpos_keys
    ).astype(jnp.bfloat16)
    ptr_values = jnp.dot(ptr_tokens, w_value, preferred_element_type=jnp.float32).astype(
        jnp.bfloat16
    )
    extra_valid = jnp.concatenate([frame + ptr_offsets >= 0, jnp.ones((1,), bool)], axis=0)
    blocks.append(
        (
            jnp.concatenate([ptr_keys, null_key], axis=0),
            jnp.concatenate([ptr_values, null_value], axis=0),
            extra_valid[None, :],
        )
    )
    mixed_rows = attend(query, blocks)
    outputs = [
        (rows_f + jnp.dot(mixed_rows, w_proj, preferred_element_type=jnp.float32)).astype(
            jnp.bfloat16
        )
    ]
    attended = jnp.stack(outputs, axis=0).reshape(frames_dev, rows_dev, columns, model_dim)
    return (attended, memory, pointers)


def put_out(*refs):
    sem = refs[-1]
    copies = [pltpu.make_async_copy(refs[k], refs[3 + k], sem.at[k]) for k in range(3)]
    for copy in copies:
        copy.start()
    for copy in copies:
        copy.wait()


def fused_body(
    features,
    masks,
    w_pix,
    mask_embed,
    w_conv,
    w_out,
    w_ptr,
    w_query,
    w_key,
    w_value,
    w_proj,
    mem_tpos,
    ptr_tpos,
    empty_memory,
):
    _, rows, columns, dim = features.shape
    frames = lax.axis_size("tm")
    mem_dim = w_key.shape[0]
    tokens = rows * columns
    half = tokens // 2
    group = stride_of(frames)
    vmem = pl.BlockSpec(memory_space=pltpu.VMEM)
    hbm = pl.BlockSpec(memory_space=pltpu.HBM)
    dma = pltpu.SemaphoreType.DMA
    results = pl.pallas_call(
        functools.partial(kernel, frames),
        out_shape=(
            pltpu.VMEM(features.shape, BF16),
            pltpu.VMEM((1, rows, columns * mem_dim), BF16),
            pltpu.VMEM((1, dim), BF16),
        ),
        in_specs=[hbm] * 14,
        out_specs=(vmem, vmem, vmem),
        scratch_shapes=[
            pltpu.VMEM((rows, columns, dim), BF16),
            pltpu.VMEM(masks.shape, masks.dtype),
            pltpu.VMEM(mask_embed.shape, BF16),
            pltpu.VMEM(mem_tpos.shape, BF16),
            pltpu.VMEM(ptr_tpos.shape, BF16),
            pltpu.VMEM(empty_memory.shape, BF16),
            pltpu.VMEM(w_pix.shape, BF16),
            pltpu.VMEM(w_conv.shape, BF16),
            pltpu.VMEM((2 * mem_dim, dim), BF16),
            pltpu.VMEM(w_ptr.shape, BF16),
            pltpu.VMEM(w_query.shape, BF16),
            pltpu.VMEM((3 * mem_dim, dim), BF16),
            pltpu.VMEM((3 * mem_dim, dim), BF16),
            pltpu.VMEM(w_proj.shape, BF16),
            pltpu.VMEM((rows + 2, columns, dim), BF16),
            pltpu.VMEM((columns, dim), BF16),
            pltpu.VMEM((tokens, dim), F32),
            pltpu.VMEM((1, dim), F32),
            pltpu.VMEM((2, group, frames // group, 1, dim), F32),
            pltpu.VMEM((tokens, 2 * mem_dim), F32),
            pltpu.VMEM((half, 2 * mem_dim), BF16),
            pltpu.VMEM((columns, 2 * mem_dim), BF16),
            pltpu.VMEM((MEMS, 2, half, 2 * mem_dim), BF16),
            dma((17,)),
            dma,
            dma,
            dma((MEMS, 2)),
            dma((MEMS, 2)),
            dma((MEMS, 2)),
            dma((MEMS, 2)),
            dma((frames // group,)),
            dma((frames // group,)),
            dma((group, 2)),
            dma((group, 2)),
        ],
        compiler_params=pltpu.CompilerParams(
            collective_id=0, has_side_effects=True
        ),
    )(
        features,
        masks,
        mask_embed,
        mem_tpos,
        ptr_tpos,
        empty_memory,
        w_pix,
        w_conv,
        w_out.T,
        w_ptr,
        w_query,
        w_key,
        w_value,
        w_proj,
    )
    return pl.pallas_call(
        put_out,
        out_shape=tuple(jax.ShapeDtypeStruct(x.shape, x.dtype) for x in results),
        in_specs=[vmem] * 3,
        out_specs=(hbm,) * 3,
        scratch_shapes=[dma((3,))],
        compiler_params=pltpu.CompilerParams(vmem_limit_bytes=2**20),
    )(*[pltpu.with_memory_space_constraint(x, pltpu.VMEM) for x in results])


def body(features, *rest):
    frames_dev, rows, columns, dim = features.shape
    key_count = MEMS * 2 * rows * columns
    fits = rows * columns * key_count * 4 <= 2**23 and rows * columns <= 256
    fits = fits and stride_of(lax.axis_size("tm")) > MEMS
    if frames_dev == 1 and lax.axis_size("space") == 2 and fits:
        return fused_body(features, *rest)
    return staged_body(features, *rest)


def solution(mesh):
    return jax.shard_map(
        body,
        mesh=mesh,
        in_specs=(P("tm", "space", None, None), P("tm", "space", None)) + (P(),) * 12,
        out_specs=(P("tm", "space", None, None), P("tm", "space", None), P("tm", None)),
        check_vma=False,
    )
```
